32 devices in a mesh: members: 2 (over y), lat: 4 (over z), lev: 2 (over x), sub: 2 (over core).
Axes of the slice: x: 2, y: 2, z: 4, core: 2. Of those that a mesh axis runs over, the one named last changes fastest.
Arguments:
- thermal_state_grid: bfloat16 [272, 512, 1024], P(('members', 'lev', 'sub'), 'lat'), parts along dimension 0, may hold values from -6 to 6
- thermal_forcing: bfloat16 [272, 512, 1024], P(('members', 'lev', 'sub'), 'lat'), parts along dimension 0, may hold values from -6 to 6
- spherical_basis_table: bfloat16 [512, 512, 512], P(('lat', 'lev', 'sub')), may hold values from -0.25 to 0.25
- implicit_solver_matrix: bfloat16 [512, 136, 136], P(('lat', 'lev', 'sub')), may hold values from -0.5 to 0.5
- fourier_order_holder: int32 [512], replicated, may hold values from 0 to 511, as said below
Outputs:
- new_temperature: bfloat16 [272, 512, 1024], P(('members', 'lev', 'sub'), 'lat'), parts along dimension 0
The draws below stay inside these ranges and needn't reach their ends.
There are 2 independent parts, one for each index of `members`. The reference program is written for one: setup_inputs(seed, part) draws one part's arguments, and reference() takes and returns one part's arrays. A program takes and returns all parts, laid end to end along the dimension named above; an argument that names none is the same for every part. Nothing has to cross between parts.
Inputs may be any that keep to these rules, and one draw needn't show every extreme that they name: fourier_order_holder is a permutation of the waves; slots 2k and 2k+1 hold waves m and 511-m for some m.
All inputs are finite; a program needn't handle non-finite values.
Results may differ from the reference program's by a relative error of at most 0.0079.
Values may be sent and summed in bfloat16 or wider, within the bound.
A program may use at most 192 MiB of HBM per device.

```python
import math
import jax
import jax.numpy as jnp
from jax import lax

MERIDIAN_TOTAL = 1024
PARALLEL_TOTAL = 512
SIGMA_LAYERS = 136
M = 512


def draw_fourier_order_holder(key, part):
    half_count = M // 2
    pair_order = jax.random.permutation(key, half_count).astype(jnp.int32)
    flipped = jax.random.randint(jax.random.fold_in(key, 7), (half_count,), 0, 2).astype(jnp.int32)
    slot_ids = jnp.arange(M, dtype=jnp.int32)
    base_wave = pair_order[slot_ids // 2]
    leading = jnp.where(flipped[slot_ids // 2] == 1, M - 1 - base_wave, base_wave)
    is_second = slot_ids % 2
    return jnp.where(is_second == 1, M - 1 - leading, leading).astype(jnp.int32)


def shard_levels(rng, dims, split, smallest, largest):
    factor_of = 1.0
    for position, blocks in split:
        heights = jax.random.uniform(jax.random.fold_in(jax.random.fold_in(rng, 6), position), (blocks,), jnp.float32, smallest / len(split), largest / len(split))
        factor_of = factor_of * jnp.repeat(jnp.exp(heights), dims[position] // blocks).reshape((-1,) + (1,) * (len(dims) - 1 - position))
    return factor_of


def bell_draw(key, dims, deviation, bound, pieces=(), kind=jnp.bfloat16):
    loudness = shard_levels(key, dims, pieces, -0.22, 0.18) if pieces else 1.0
    array = jax.random.normal(key, dims, jnp.float32) * deviation * loudness
    return jnp.minimum(jnp.maximum(array, -bound), bound).astype(kind)


def setup_inputs(seed: int = 0, part: int = 0) -> dict:
    splits = jax.random.split(jax.random.key(seed), 6)
    part_splits = jax.random.split(jax.random.fold_in(splits[5], part), 6)
    thermal_state_grid = bell_draw(part_splits[0], (SIGMA_LAYERS, PARALLEL_TOTAL, MERIDIAN_TOTAL), 1.0, 6.0, ((0, 4), (1, 4)))
    thermal_forcing = bell_draw(part_splits[1], (SIGMA_LAYERS, PARALLEL_TOTAL, MERIDIAN_TOTAL), 1.0, 6.0, ((0, 4), (1, 4)))
    spherical_basis_table = bell_draw(splits[2], (M, PARALLEL_TOTAL, M), PARALLEL_TOTAL ** -0.5, 0.25, ((0, 16),))
    implicit_solver_matrix = bell_draw(splits[3], (M, SIGMA_LAYERS, SIGMA_LAYERS), SIGMA_LAYERS ** -0.5, 0.5, ((0, 16),))
    fourier_order_holder = draw_fourier_order_holder(jax.random.fold_in(splits[5], 71), part)
    return {"thermal_state_grid": thermal_state_grid, "thermal_forcing": thermal_forcing, "spherical_basis_table": spherical_basis_table, "implicit_solver_matrix": implicit_solver_matrix, "fourier_order_holder": fourier_order_holder}


block_slots = 16

def raw_table(fourier_order_holder, lon_count):
    meridian_position = jnp.arange(lon_count, dtype=jnp.int32)
    phases = meridian_position[:, None] * fourier_order_holder[None, :].astype(jnp.int32) % lon_count
    angles = phases.astype(jnp.float32) * (2.0 * math.pi / lon_count)
    factor = 1.0 / math.sqrt(lon_count)
    stacked = jnp.stack([jnp.cos(angles), -jnp.sin(angles)], axis=2)
    return stacked.reshape(lon_count, 2 * fourier_order_holder.shape[0]) * factor

def reference(thermal_state_grid, thermal_forcing, spherical_basis_table, implicit_solver_matrix, fourier_order_holder):
    present_state = thermal_state_grid.astype(jnp.float32)
    explicit = (present_state + 0.5 * thermal_forcing.astype(jnp.float32) - 0.3 * present_state * present_state * present_state / (1.0 + present_state * present_state)).astype(jnp.bfloat16)
    raw = raw_table(fourier_order_holder, MERIDIAN_TOTAL)
    analysis = raw.astype(jnp.bfloat16)
    weights = jnp.where(fourier_order_holder == 0, 1.0, 2.0).astype(jnp.float32)
    synthesis = (raw.T * jnp.repeat(weights, 2)[:, None]).astype(jnp.bfloat16)
    spectral = jnp.dot(explicit.reshape(SIGMA_LAYERS * PARALLEL_TOTAL, MERIDIAN_TOTAL), analysis, preferred_element_type=jnp.float32).astype(jnp.bfloat16)
    groups = M // block_slots
    spec_blocks = spectral.reshape(SIGMA_LAYERS, PARALLEL_TOTAL, groups, block_slots, 2).transpose(2, 0, 1, 3, 4)
    leg_blocks = spherical_basis_table.reshape(groups, block_slots, PARALLEL_TOTAL, M)

    def forward_group(operands):
        return jnp.einsum('lxsc,sxn->lscn', operands[0].astype(jnp.float32), operands[1].astype(jnp.float32)).astype(jnp.bfloat16)
    coeffs = lax.map(forward_group, (spec_blocks, leg_blocks))
    coeffs = coeffs.transpose(1, 0, 2, 3, 4).reshape(SIGMA_LAYERS, M, 2, M)
    solved = jnp.einsum('skl,lscn->kscn', implicit_solver_matrix.astype(jnp.float32), coeffs.astype(jnp.float32))
    degrees = jnp.arange(M, dtype=jnp.int32)
    live_mask = degrees[None, :] >= fourier_order_holder[:, None]
    solved = jnp.where(live_mask[None, :, None, :], solved, 0.0).astype(jnp.bfloat16)
    solved_blocks = solved.reshape(SIGMA_LAYERS, groups, block_slots, 2, M).transpose(1, 0, 2, 3, 4)

    def inverse_group(operands):
        return jnp.einsum('sxn,lscn->lxsc', operands[1].astype(jnp.float32), operands[0].astype(jnp.float32)).astype(jnp.bfloat16)
    synthesized = lax.map(inverse_group, (solved_blocks, leg_blocks))
    synthesized = synthesized.transpose(1, 2, 0, 3, 4).reshape(SIGMA_LAYERS * PARALLEL_TOTAL, 2 * M)
    result = jnp.dot(synthesized, synthesis, preferred_element_type=jnp.float32).astype(jnp.bfloat16)
    return result.reshape(SIGMA_LAYERS, PARALLEL_TOTAL, MERIDIAN_TOTAL)
```

```python
import functools
import math

import jax
import jax.numpy as jnp
from jax import lax
from jax.experimental import pallas as pl
from jax.experimental.pallas import tpu as pltpu
from jax.sharding import PartitionSpec as P

CHUNKS = 4
GROUP = 8
STEP = 2
CAPS = (1024, 0)
OWNERS = ("lat", "lev", "sub")


def raw_table(waves, lon_count):
    meridian = jnp.arange(lon_count, dtype=jnp.int32)
    phases = waves[:, None] * meridian[None, :] % lon_count
    angles = phases.astype(jnp.float32) * (2.0 * math.pi / lon_count)
    factor = 1.0 / math.sqrt(lon_count)
    return jnp.stack([jnp.cos(angles), -jnp.sin(angles)], axis=1) * factor


def place(peer, level_parts):
    subs = lax.axis_size("sub")
    return {
        "lat": peer // level_parts,
        "lev": (peer % level_parts) // subs,
        "sub": peer % subs,
    }


def my_place(level_parts):
    subs = lax.axis_size("sub")
    return lax.axis_index("lat") * level_parts + lax.axis_index("lev") * subs + lax.axis_index("sub")


def fused_kernel(
    n, level_parts, cap,
    state, forcing, basis, solver, near, far, alive, order, key, who,
    land, land_t, back, synthesis,
    table, buf, basis_v, solver_v, got, wide, rows, mix, split, st, fo,
    packed, other, acc, solved_f, part_out, part_in, solved_out, solved_in,
    fs, fr, bs, br, ts, tr, ms, mr, loc, ins,
):
    levels, lats, lons = state.shape
    chunks, _, _, pairs, _ = buf.shape
    slots, lat_total, degrees = basis.shape
    total = levels * level_parts
    lat_parts = n // level_parts
    steps = levels // STEP
    tile = near.shape[2]
    mine = my_place(level_parts)
    lat, group, sub = mine // level_parts, mine % level_parts, lax.axis_index("sub")
    half_n = n // 2
    half, seat = mine // half_n, mine % half_n
    mirror = (mine + half_n) % n
    half_lats = lat_total // 2
    upper = degrees // 2

    def remote(src, dst, send_sem, recv_sem, peer):
        return pltpu.make_async_remote_copy(
            src_ref=src,
            dst_ref=dst,
            send_sem=send_sem,
            recv_sem=recv_sem,
            device_id=place(peer, level_parts),
            device_id_type=pl.DeviceIdType.MESH,
        )

    def loop(count, body):
        def run(i, carry):
            body(i)
            return carry

        lax.fori_loop(0, count, run, 0)

    def forward(c, peer, landing, cut):
        return remote(
            buf.at[(c, peer, *cut)], land.at[(c, landing, *cut)], fs.at[c, peer], fr.at[c, landing], peer
        )

    def forward_own(c, cut):
        return pltpu.make_async_copy(buf.at[(c, mine, *cut)], land.at[(c, mine, *cut)], loc.at[0, c])

    def backward(c, peer, landing):
        return remote(buf.at[c, peer], back.at[c, landing], bs.at[c, peer], br.at[c, landing], peer)

    def backward_own(c):
        return pltpu.make_async_copy(buf.at[c, mine], back.at[c, mine], loc.at[1, c])

    def in_turn(start):
        def one(t):
            turn = (lat + t // level_parts + (1 - sub) * (lat_parts // 2)) % lat_parts
            peer = turn * level_parts + (group + t) % level_parts

            @pl.when(peer != mine)
            def _():
                start(peer)

        loop(n, one)

    def others(wait):
        loop(n - 1, lambda d: wait((mine + 1 + d) % n))

    def push(c, cut):
        in_turn(lambda peer: forward(c, peer, mine, cut).start())
        forward_own(c, cut).start()

    def narrow(o, kind, place_in):
        return remote(
            buf.at[0, o], land_t.at[kind, place_in], ts.at[o], tr.at[kind, place_in], half * half_n + o % half_n
        )

    def narrow_own(kind):
        owner = ((half + kind) % 2) * half_n + seat
        return pltpu.make_async_copy(buf.at[0, owner], land_t.at[kind, seat], loc.at[2, kind])

    def narrow_back(kind, to, owner):
        return remote(
            buf.at[0, kind * half_n + to], back.at[0, owner], bs.at[0, kind * half_n + to], br.at[0, owner],
            half * half_n + to,
        )

    def narrow_back_own(kind):
        owner = ((half + kind) % 2) * half_n + seat
        return pltpu.make_async_copy(buf.at[0, kind * half_n + seat], back.at[0, owner], loc.at[3, kind])

    def seats(do):
        def one(d):
            do((seat + 1 + d) % half_n)

        loop(half_n - 1, one)

    def trig(a):
        return far[0, :, a : a + 1] * near[0] - far[1, :, a : a + 1] * near[1]

    def fetch(i):
        slot = i % 2
        cut = pl.ds(i * STEP, STEP)
        return (
            pltpu.make_async_copy(state.at[cut], st.at[slot], ins.at[0, slot]),
            pltpu.make_async_copy(forcing.at[cut], fo.at[slot], ins.at[1, slot]),
        )

    weights = (
        pltpu.make_async_copy(basis, basis_v, ins.at[2, 0]),
        pltpu.make_async_copy(solver, solver_v, ins.at[2, 1]),
    )

    for copy in fetch(0):
        copy.start()
    barrier = pltpu.get_barrier_semaphore()
    others(
        lambda peer: pl.semaphore_signal(
            barrier, inc=1, device_id=place(peer, level_parts), device_id_type=pl.DeviceIdType.MESH
        )
    )
    for a in range(lons // tile):
        table[:, a * tile : (a + 1) * tile] = trig(a).astype(jnp.bfloat16)

    lead = 1 if cap else 0

    def dft(i):
        for copy in fetch(i):
            copy.wait()

        @pl.when(i + 1 < steps)
        def _():
            for copy in fetch(i + 1):
                copy.start()

        slot = i % 2
        present = st[slot].astype(jnp.float32)
        explicit = (
            present
            + 0.5 * fo[slot].astype(jnp.float32)
            - 0.3 * present * present * present / (1.0 + present * present)
        ).astype(jnp.bfloat16)
        spectral = lax.dot_general(
            table[...],
            explicit.reshape(STEP * lats, lons),
            (((1,), (1,)), ((), ())),
            preferred_element_type=jnp.float32,
        ).astype(jnp.bfloat16)
        spectral = spectral.reshape(chunks, n, pairs, STEP * lats)
        for level in range(STEP):
            buf[:, :, i * STEP + level] = spectral[..., level * lats : (level + 1) * lats]

        @pl.when(i == 0)
        def _():
            pl.semaphore_wait(barrier, n - 1)
            for copy in weights:
                copy.start()

        push(lead, (pl.ds(i * STEP, STEP),))

    loop(steps, dft)
    for copy in weights:
        copy.wait()

    if cap:
        lanes = packed.shape[1]
        place_of = lax.broadcasted_iota(jnp.int32, (upper, lanes), 0)
        packed[...] = jnp.zeros_like(packed)

        def pack(w):
            pick = (place_of + w * upper == key[...]).astype(jnp.float32).astype(jnp.bfloat16)
            part = jnp.dot(
                basis_v[order[w], :, upper:], pick, preferred_element_type=jnp.float32
            )
            packed[...] = (packed[...].astype(jnp.float32) + part).astype(jnp.bfloat16)

        loop(GROUP, pack)
        far_rows = pl.ds(pl.multiple_of((1 - half) * half_lats, half_lats), half_lats)
        near_rows = pl.ds(pl.multiple_of(half * half_lats, half_lats), half_lats)
        give_rows = remote(packed.at[far_rows], other, ms.at[0], mr.at[0], mirror)
        give_rows.start()

        def narrow_start(d):
            o = (mine + half_n + d) % n

            @pl.when(o % half_n != seat)
            def _():
                narrow(o, (o // half_n + half) % 2, seat).start()

        loop(n, narrow_start)
        for kind in range(2):
            narrow_own(kind).start()
    for c in range(lead + 1, chunks):
        push(c, ())

    for a in range(lons // tile):
        table[:, a * tile : (a + 1) * tile] = (trig(a) * far[2, :, a : a + 1]).astype(jnp.bfloat16)
    give_table = pltpu.make_async_copy(table, synthesis, loc.at[4, 0])
    give_table.start()

    def take(source, bands):
        landed = pltpu.make_async_copy(source, got.at[pl.ds(0, bands * level_parts)], loc.at[4, 1])
        landed.start()
        landed.wait()

        def gather(q):
            at = pl.ds(pl.multiple_of(q * lats, lats), lats)
            for g in range(level_parts):
                wide[g] = got[q * level_parts + g].astype(jnp.float32).reshape(levels * pairs, lats)
                for k in range(pairs):
                    rows[k, pl.ds(g * levels, levels), at] = wide[g, pl.ds(k, levels, stride=pairs), :]

        loop(bands, gather)

    def spread(s, bands):
        for q in range(bands):
            for g in range(level_parts):
                for c in range(2):
                    split[q * level_parts + g, pl.ds(2 * s + c, levels, stride=pairs), :] = mix[
                        pl.ds(c * total + g * levels, levels), q * lats : (q + 1) * lats
                    ]

    def whole(c):
        others(lambda peer: forward(c, mine, peer, ()).wait_recv())
        forward_own(c, ()).wait()
        take(land.at[c], lat_parts)
        low = upper if cap and c < slots // 2 // GROUP else 0

        def slot(s):
            here = order[c * GROUP + s]
            legendre = basis_v[here, :, low:]
            columns = rows[pl.ds(2 * s, 2)].reshape(2 * total, lat_total).astype(jnp.bfloat16)
            coeffs = jnp.dot(columns, legendre, preferred_element_type=jnp.float32)
            mask = alive[c * GROUP + s][:, low:] > 0.5
            solved = []
            for k in range(2):
                part = coeffs[k * total : (k + 1) * total].astype(jnp.bfloat16)
                part = jnp.dot(solver_v[here], part, preferred_element_type=jnp.float32)
                solved.append(jnp.where(mask, part, 0.0))
            solved = jnp.concatenate(solved, axis=0).astype(jnp.bfloat16)
            mix[...] = lax.dot_general(
                solved, legendre, (((1,), (1,)), ((), ())), preferred_element_type=jnp.float32
            )
            spread(s, lat_parts)

        loop(GROUP, slot)
        others(lambda peer: forward(c, peer, mine, ()).wait_send())

        def fill(peer):
            buf[c, peer] = split[peer].astype(jnp.bfloat16).reshape(levels, pairs, lats)

        fill(mine)
        backward_own(c).start()

        def send(peer):
            fill(peer)
            backward(c, peer, mine).start()

        in_turn(send)

    def narrow_coeffs(kind, legendre):
        seats(lambda j: narrow(j, kind, j).wait_recv())
        narrow_own(kind).wait()
        take(land_t.at[kind], lat_parts // 2)
        acc[...] = jnp.zeros_like(acc)

        def one(w):
            columns = rows[pl.ds(2 * w, 2), :, :half_lats].reshape(2 * total, half_lats).astype(jnp.bfloat16)
            part = jnp.dot(columns, legendre(), preferred_element_type=jnp.float32)
            acc[...] = jnp.where(who[kind] == w, part, acc[...])

        loop(GROUP, one)

    def narrow_synthesis(kind, source, legendre):
        def one(w):
            solved = jnp.where(who[kind] == w, source[...].astype(jnp.float32), 0.0).astype(jnp.bfloat16)
            mix[:, :half_lats] = lax.dot_general(
                solved, legendre(), (((1,), (1,)), ((), ())), preferred_element_type=jnp.float32
            )
            spread(w, lat_parts // 2)

        loop(GROUP, one)

        def fill(j):
            buf[0, kind * half_n + j] = split[j].astype(jnp.bfloat16).reshape(levels, pairs, lats)

        owner = mine if kind == 0 else mirror
        fill(seat)
        narrow_back_own(kind).start()

        def send(j):
            fill(j)
            narrow_back(kind, j, owner).start()

        seats(send)

    if cap:
        give_part = remote(part_out, part_in, ms.at[1], mr.at[1], mirror)
        give_solved = remote(solved_out, solved_in, ms.at[2], mr.at[2], mirror)
        whole(1)
        give_rows.wait_recv()
        narrow_coeffs(1, lambda: other[...])
        part_out[...] = acc[...].astype(jnp.bfloat16)
        give_part.start()
        whole(2)
        narrow_coeffs(0, lambda: packed[near_rows])
        give_part.wait_recv()
        acc[...] += part_in[...].astype(jnp.float32)

        def solve(w):
            for k in range(2):
                at = pl.ds(k * total, total)
                part = jnp.dot(
                    solver_v[order[w]], acc[at].astype(jnp.bfloat16), preferred_element_type=jnp.float32
                )
                split_at = who[0] == w
                solved_f[at] = jnp.where(split_at, part, solved_f[at])

        solved_f[...] = jnp.zeros_like(solved_f)
        loop(GROUP, solve)
        solved_out[...] = solved_f[...].astype(jnp.bfloat16)
        give_solved.start()

        def narrow_sent(d):
            o = (mine + half_n + d) % n

            @pl.when(o % half_n != seat)
            def _():
                narrow(o, (o // half_n + half) % 2, seat).wait_send()

        loop(n, narrow_sent)
        narrow_synthesis(0, solved_out, lambda: packed[near_rows])
        for c in range(3, chunks):
            whole(c)
        give_solved.wait_recv()
        narrow_synthesis(1, solved_in, lambda: other[...])
        for copy in (give_rows, give_part, give_solved):
            copy.wait_send()
        for kind in range(2):
            owner = mine if kind == 0 else mirror
            narrow_back_own(kind).wait()
            seats(lambda j, kind=kind, owner=owner: narrow_back(kind, j, owner).wait_send())

            def arrived(j, kind=kind):
                narrow_back(kind, j, ((half + kind) % 2) * half_n + j).wait_recv()

            seats(arrived)
    else:
        for c in range(chunks):
            whole(c)
    for c in range(lead, chunks):
        others(lambda peer, c=c: backward(c, peer, mine).wait_send())
        others(lambda peer, c=c: backward(c, mine, peer).wait_recv())
        backward_own(c).wait()
    give_table.wait()


def fused(state, forcing, basis, solver, near, far, alive, order, key, who, n, level_parts, cap, number):
    levels, lats, lons = state.shape
    slots, lat_total, degrees = basis.shape
    total = solver.shape[1]
    pairs = 2 * GROUP
    chunks = slots // GROUP
    table_rows = near.shape[1]
    lanes = cap if cap else 128
    half_lats = lat_total // 2
    some = lambda *shape: shape if cap else (16, 128)
    message = (levels, pairs, lats)
    vmem = pl.BlockSpec(memory_space=pltpu.VMEM)
    hbm = pl.BlockSpec(memory_space=pl.ANY)
    smem = pl.BlockSpec(memory_space=pltpu.SMEM)
    short = (16, 16, 128)
    bf16, f32 = jnp.bfloat16, jnp.float32
    _, _, back, synthesis = pl.pallas_call(
        functools.partial(fused_kernel, n, level_parts, cap),
        out_shape=(
            jax.ShapeDtypeStruct((chunks, n, *message), bf16),
            jax.ShapeDtypeStruct((2, n // 2, *(message if cap else short)), bf16),
            jax.ShapeDtypeStruct((chunks, n, *message), bf16),
            jax.ShapeDtypeStruct((table_rows, lons), bf16),
        ),
        in_specs=[hbm, hbm, hbm, hbm, vmem, vmem, vmem, smem, vmem, vmem],
        out_specs=(hbm, hbm, hbm, hbm),
        scratch_shapes=[
            pltpu.VMEM((table_rows, lons), bf16),
            pltpu.VMEM((chunks, n, *message), bf16),
            pltpu.VMEM(basis.shape, bf16),
            pltpu.VMEM(solver.shape, bf16),
            pltpu.VMEM((n, *message), bf16),
            pltpu.VMEM((level_parts, levels * pairs, lats), f32),
            pltpu.VMEM((pairs, total, lat_total), f32),
            pltpu.VMEM((2 * total, lat_total), f32),
            pltpu.VMEM((n, levels * pairs, lats), f32),
            pltpu.VMEM((2, STEP, lats, lons), bf16),
            pltpu.VMEM((2, STEP, lats, lons), bf16),
            pltpu.VMEM(some(lat_total, lanes), bf16),
            pltpu.VMEM(some(half_lats, lanes), bf16),
            pltpu.VMEM(some(2 * total, lanes), f32),
            pltpu.VMEM(some(2 * total, lanes), f32),
            pltpu.VMEM(some(2 * total, lanes), bf16),
            pltpu.VMEM(some(2 * total, lanes), bf16),
            pltpu.VMEM(some(2 * total, lanes), bf16),
            pltpu.VMEM(some(2 * total, lanes), bf16),
            pltpu.SemaphoreType.DMA((chunks, n)),
            pltpu.SemaphoreType.DMA((chunks, n)),
            pltpu.SemaphoreType.DMA((chunks, n)),
            pltpu.SemaphoreType.DMA((chunks, n)),
            pltpu.SemaphoreType.DMA((n,)),
            pltpu.SemaphoreType.DMA((2, n // 2)),
            pltpu.SemaphoreType.DMA((3,)),
            pltpu.SemaphoreType.DMA((3,)),
            pltpu.SemaphoreType.DMA((5, max(chunks, 2))),
            pltpu.SemaphoreType.DMA((3, 2)),
        ],
        compiler_params=pltpu.CompilerParams(
            collective_id=number, has_side_effects=True, vmem_limit_bytes=61 << 20
        ),
    )(state, forcing, basis, solver, near, far, alive, order, key, who)
    return back, synthesis

def small_tables(waves, lon_count, tile):
    waves = jnp.repeat(waves, 2)[:, None]
    quarter = (jnp.arange(waves.shape[0], dtype=jnp.int32) % 2)[:, None] * (lon_count // 4)
    unit = 2.0 * math.pi / lon_count
    fine = jnp.arange(tile, dtype=jnp.int32)[None, :] * waves % lon_count
    coarse = jnp.arange(lon_count // tile, dtype=jnp.int32)[None, :] * tile * waves + quarter
    fine, coarse = fine.astype(jnp.float32) * unit, (coarse % lon_count).astype(jnp.float32) * unit
    factor = 1.0 / math.sqrt(lon_count)
    weights = jnp.broadcast_to(jnp.where(waves == 0, 1.0, 2.0), coarse.shape)
    near = jnp.stack([jnp.cos(fine), jnp.sin(fine)])
    far = jnp.stack([jnp.cos(coarse) * factor, jnp.sin(coarse) * factor, weights])
    return near, far


def slot_order(waves, n):
    mine = waves.reshape(n, -1)
    slots = mine.shape[1]
    rank = jnp.sum((mine[:, None, :] > mine[:, :, None]).astype(jnp.int32), axis=2)
    here = rank[:, :, None] == jnp.arange(slots, dtype=jnp.int32)
    ranked = jnp.sum(jnp.where(here, mine[:, :, None], 0), axis=1)
    order = jnp.sum(jnp.where(here, jnp.arange(slots, dtype=jnp.int32)[None, :, None], 0), axis=1)
    return ranked, order


def packing(ranked, degrees, lanes):
    first = ranked[:, :GROUP]
    counts = degrees - first
    before = jnp.arange(GROUP)[:, None] > jnp.arange(GROUP)[None, :]
    starts = jnp.sum(jnp.where(before, counts[:, None, :], 0), axis=2)
    lane = jnp.arange(lanes, dtype=jnp.int32)
    inside = (lane >= starts[:, :, None]) & (lane < (starts + counts)[:, :, None])
    upper = degrees // 2
    wave = jnp.arange(GROUP, dtype=jnp.int32)[None, :, None]
    column = wave * upper + first[:, :, None] - upper + lane - starts[:, :, None]
    key = jnp.sum(jnp.where(inside, column + 1, 0), axis=1) - 1
    who = jnp.sum(jnp.where(inside, wave + 1, 0), axis=1) - 1
    return key, who


def fast(state, forcing, basis, solver, waves, lat_parts, level_parts):
    levels, lats, lons = state.shape
    slots, _, degrees = basis.shape
    n = lat_parts * level_parts
    chunks = slots // GROUP
    owner = lax.axis_index(OWNERS)

    mirror = (owner + n // 2) % n
    ranked, order = slot_order(waves, n)
    flat = ranked.reshape(n, chunks, GROUP).transpose(1, 0, 2).reshape(-1)
    near, far = small_tables(flat, lons, 128)
    mine = lax.dynamic_index_in_dim(ranked, owner, 0, keepdims=False)
    live = jnp.arange(degrees, dtype=jnp.int32)[None, :] >= mine[:, None]
    alive = live.astype(jnp.float32)[:, None, :]
    order = lax.dynamic_index_in_dim(order, owner, 0, keepdims=False)

    def branch(number):
        cap = CAPS[number]

        def run(operands):
            both = jnp.stack(
                [lax.dynamic_index_in_dim(ranked, o, 0, keepdims=False) for o in (owner, mirror)]
            )
            key, who = packing(both, degrees, max(cap, 128))
            return fused(*operands, key[:1], who[:, None], n, level_parts, cap, number)

        return run

    needed = jnp.max(jnp.sum(degrees - ranked[:, :GROUP], axis=1))
    unfit = sum((needed > cap).astype(jnp.int32) for cap in CAPS if cap)
    back, synthesis = lax.switch(
        unfit,
        [branch(number) for number in range(len(CAPS))],
        (state, forcing, basis, solver, near, far, alive, order),
    )
    synthesis = synthesis.reshape(chunks, n, 2 * GROUP, lons)
    result = jnp.einsum("holkx,hokj->lxj", back, synthesis, preferred_element_type=jnp.float32)
    return result.astype(jnp.bfloat16)


def make_shards(lat_parts, level_parts):
    owners = lat_parts * level_parts

    def shards(state, forcing, basis, solver, waves):
        levels, lats, lons = state.shape
        slots, lat_total, degrees = basis.shape
        level_total = solver.shape[1]
        owner = lax.axis_index(OWNERS)
        my_waves = lax.dynamic_slice_in_dim(waves, owner * slots, slots)
        live = jnp.arange(degrees, dtype=jnp.int32)[None, :] >= my_waves[:, None]
        if (
            lats % 128 == 0
            and lons % 512 == 0
            and slots % (4 * GROUP) == 0
            and levels % STEP == 0
            and lat_parts % 2 == 0
        ):
            return fast(state, forcing, basis, solver, waves, lat_parts, level_parts)
        present = state.astype(jnp.float32)
        explicit = (
            present
            + 0.5 * forcing.astype(jnp.float32)
            - 0.3 * present * present * present / (1.0 + present * present)
        ).astype(jnp.bfloat16)
        raw = raw_table(waves, lons)
        analysis = raw.astype(jnp.bfloat16)
        weights = jnp.where(waves == 0, 1.0, 2.0).astype(jnp.float32)
        synthesis = (raw * weights[:, None, None]).astype(jnp.bfloat16)
        chunks = CHUNKS
        part = slots // chunks
        analysis = analysis.reshape(owners, slots, 2, lons)
        synthesis = synthesis.reshape(owners, slots, 2, lons)
        sent = []
        for i in range(chunks):
            own = slice(i * part, (i + 1) * part)
            spectral = jnp.einsum(
                "oscj,lxj->osclx", analysis[:, own], explicit, preferred_element_type=jnp.float32
            ).astype(jnp.bfloat16)
            sent.append(lax.all_to_all(spectral, OWNERS, split_axis=0, concat_axis=0, tiled=True))
        back = []
        for i in range(chunks):
            own = slice(i * part, (i + 1) * part)
            got = sent[i].reshape(lat_parts, level_parts, part, 2, levels, lats)
            table = basis[own]
            columns = got.transpose(2, 3, 1, 4, 0, 5).reshape(part, 2 * level_total, lat_total)
            coeffs = jnp.einsum(
                "srx,sxn->srn", columns, table, preferred_element_type=jnp.float32
            ).astype(jnp.bfloat16).reshape(part, 2, level_total, degrees)
            solved = jnp.einsum(
                "skl,scln->sckn", solver[own], coeffs, preferred_element_type=jnp.float32
            )
            solved = jnp.where(live[own][:, None, None, :], solved, 0.0).astype(jnp.bfloat16)
            grid = jnp.einsum(
                "srn,sxn->srx",
                solved.reshape(part, 2 * level_total, degrees),
                table,
                preferred_element_type=jnp.float32,
            ).astype(jnp.bfloat16)
            grid = grid.reshape(part, 2, level_parts, levels, lat_parts, lats)
            grid = grid.transpose(4, 2, 0, 1, 3, 5).reshape(owners, part, 2, levels, lats)
            back.append(lax.all_to_all(grid, OWNERS, split_axis=0, concat_axis=0, tiled=True))
        waved = jnp.concatenate(back, axis=1)
        result = jnp.einsum(
            "osclx,oscj->lxj", waved, synthesis, preferred_element_type=jnp.float32
        )
        return result.astype(jnp.bfloat16)

    return shards


def solution(mesh):
    lat_parts = mesh.shape["lat"]
    level_parts = mesh.shape["lev"] * mesh.shape["sub"]
    return jax.shard_map(
        make_shards(lat_parts, level_parts),
        mesh=mesh,
        in_specs=(
            P(("members", "lev", "sub"), "lat", None),
            P(("members", "lev", "sub"), "lat", None),
            P(OWNERS, None, None),
            P(OWNERS, None, None),
            P(),
        ),
        out_specs=P(("members", "lev", "sub"), "lat", None),
        check_vma=False,
    )
```

```python
import functools
import math

import jax
import jax.numpy as jnp
from jax import lax
from jax.experimental import pallas as pl
from jax.experimental.pallas import tpu as pltpu
from jax.sharding import PartitionSpec as P

CHUNKS = 4
GROUP = 8
STEP = 2
CAPS = (1024, 0)
OWNERS = ("lat", "lev", "sub")


def raw_table(waves, lon_count):
    meridian = jnp.arange(lon_count, dtype=jnp.int32)
    phases = waves[:, None] * meridian[None, :] % lon_count
    angles = phases.astype(jnp.float32) * (2.0 * math.pi / lon_count)
    factor = 1.0 / math.sqrt(lon_count)
    return jnp.stack([jnp.cos(angles), -jnp.sin(angles)], axis=1) * factor


def place(peer, level_parts):
    subs = lax.axis_size("sub")
    return {
        "lat": peer // level_parts,
        "lev": (peer % level_parts) // subs,
        "sub": peer % subs,
    }


def my_place(level_parts):
    subs = lax.axis_size("sub")
    return lax.axis_index("lat") * level_parts + lax.axis_index("lev") * subs + lax.axis_index("sub")


def fused_kernel(
    n, level_parts, cap,
    state, forcing, basis, solver, near, far, alive, order, key, who,
    land, land_t, back, synthesis,
    table, buf, basis_v, solver_v, got, wide, rows, mix, split, st, fo,
    packed, given, relay, passed, other, acc, solved_f, part_out, part_in, solved_out, solved_in,
    fs, fr, bs, br, ts, tr, ms, mr, loc, ins,
):
    levels, lats, lons = state.shape
    chunks, _, _, pairs, _ = buf.shape
    slots, lat_total, degrees = basis.shape
    total = levels * level_parts
    lat_parts = n // level_parts
    steps = levels // STEP
    tile = near.shape[2]
    mine = my_place(level_parts)
    lat, group, sub = mine // level_parts, mine % level_parts, lax.axis_index("sub")
    half_n = n // 2
    half, seat = mine // half_n, mine % half_n
    mirror = (mine + half_n) % n
    member, members = lax.axis_index("members"), lax.axis_size("members")
    half_lats = lat_total // 2
    upper = degrees // 2

    def remote(src, dst, send_sem, recv_sem, peer):
        return pltpu.make_async_remote_copy(
            src_ref=src,
            dst_ref=dst,
            send_sem=send_sem,
            recv_sem=recv_sem,
            device_id=place(peer, level_parts),
            device_id_type=pl.DeviceIdType.MESH,
        )

    def loop(count, body):
        def run(i, carry):
            body(i)
            return carry

        lax.fori_loop(0, count, run, 0)

    def forward(c, peer, landing, cut):
        return remote(
            buf.at[(c, peer, *cut)], land.at[(c, landing, *cut)], fs.at[c, peer], fr.at[c, landing], peer
        )

    def forward_own(c, cut):
        return pltpu.make_async_copy(buf.at[(c, mine, *cut)], land.at[(c, mine, *cut)], loc.at[0, c])

    def backward(c, peer, landing):
        return remote(buf.at[c, peer], back.at[c, landing], bs.at[c, peer], br.at[c, landing], peer)

    def backward_own(c):
        return pltpu.make_async_copy(buf.at[c, mine], back.at[c, mine], loc.at[1, c])

    def in_turn(start):
        def one(t):
            turn = (lat + t // level_parts + (1 - sub) * (lat_parts // 2)) % lat_parts
            peer = turn * level_parts + (group + t) % level_parts

            @pl.when(peer != mine)
            def _():
                start(peer)

        loop(n, one)

    def others(wait):
        loop(n - 1, lambda d: wait((mine + 1 + d) % n))

    def push(c, cut):
        in_turn(lambda peer: forward(c, peer, mine, cut).start())
        forward_own(c, cut).start()

    def narrow(o, kind, place_in):
        return remote(
            buf.at[0, o], land_t.at[kind, place_in], ts.at[o], tr.at[kind, place_in], half * half_n + o % half_n
        )

    def narrow_own(kind):
        owner = ((half + kind) % 2) * half_n + seat
        return pltpu.make_async_copy(buf.at[0, owner], land_t.at[kind, seat], loc.at[2, kind])

    def narrow_back(kind, to, owner):
        return remote(
            buf.at[0, kind * half_n + to], back.at[0, owner], bs.at[0, kind * half_n + to], br.at[0, owner],
            half * half_n + to,
        )

    def narrow_back_own(kind):
        owner = ((half + kind) % 2) * half_n + seat
        return pltpu.make_async_copy(buf.at[0, kind * half_n + seat], back.at[0, owner], loc.at[3, kind])

    def seats(do):
        def one(d):
            do((seat + 1 + d) % half_n)

        loop(half_n - 1, one)

    def trig(a):
        return far[0, :, a : a + 1] * near[0] - far[1, :, a : a + 1] * near[1]

    def fetch(i):
        slot = i % 2
        cut = pl.ds(i * STEP, STEP)
        return (
            pltpu.make_async_copy(state.at[cut], st.at[slot], ins.at[0, slot]),
            pltpu.make_async_copy(forcing.at[cut], fo.at[slot], ins.at[1, slot]),
        )

    weights = (
        pltpu.make_async_copy(basis, basis_v, ins.at[2, 0]),
        pltpu.make_async_copy(solver, solver_v, ins.at[2, 1]),
    )

    for copy in fetch(0):
        copy.start()
    barrier = pltpu.get_barrier_semaphore()
    others(
        lambda peer: pl.semaphore_signal(
            barrier, inc=1, device_id=place(peer, level_parts), device_id_type=pl.DeviceIdType.MESH
        )
    )
    def twin(d):
        return dict(place(mine, level_parts), members=(member + d) % members)

    if cap:
        for d in range(1, members):
            pl.semaphore_signal(
                barrier, inc=1, device_id=twin(d), device_id_type=pl.DeviceIdType.MESH
            )
    greeted = n - 1 + (members - 1 if cap else 0)
    for a in range(lons // tile):
        table[:, a * tile : (a + 1) * tile] = trig(a).astype(jnp.bfloat16)

    lead = 1 if cap else 0

    def dft(i):
        for copy in fetch(i):
            copy.wait()

        @pl.when(i + 1 < steps)
        def _():
            for copy in fetch(i + 1):
                copy.start()

        slot = i % 2
        present = st[slot].astype(jnp.float32)
        explicit = (
            present
            + 0.5 * fo[slot].astype(jnp.float32)
            - 0.3 * present * present * present / (1.0 + present * present)
        ).astype(jnp.bfloat16)
        spectral = lax.dot_general(
            table[...],
            explicit.reshape(STEP * lats, lons),
            (((1,), (1,)), ((), ())),
            preferred_element_type=jnp.float32,
        ).astype(jnp.bfloat16)
        spectral = spectral.reshape(chunks, n, pairs, STEP * lats)
        for level in range(STEP):
            buf[:, :, i * STEP + level] = spectral[..., level * lats : (level + 1) * lats]

        @pl.when(i == 0)
        def _():
            pl.semaphore_wait(barrier, greeted)
            for copy in weights:
                copy.start()

        push(lead, (pl.ds(i * STEP, STEP),))

    loop(steps, dft)
    for copy in weights:
        copy.wait()

    if cap:
        lanes = packed.shape[1]
        place_of = lax.broadcasted_iota(jnp.int32, (upper, lanes), 0)
        packed[...] = jnp.zeros_like(packed)

        def pack(w):
            pick = (place_of + w * upper == key[...]).astype(jnp.float32).astype(jnp.bfloat16)
            part = jnp.dot(
                basis_v[order[w], :, upper:], pick, preferred_element_type=jnp.float32
            )
            packed[...] = (packed[...].astype(jnp.float32) + part).astype(jnp.bfloat16)

        loop(GROUP, pack)
        share = half_lats // members
        far_share = pl.ds(pl.multiple_of((1 - half) * half_lats + member * share, share), share)
        near_rows = pl.ds(pl.multiple_of(half * half_lats, half_lats), half_lats)
        give_rows = remote(packed.at[far_share], given, ms.at[0], mr.at[0], mirror)
        give_rows.start()

        def narrow_start(d):
            o = (mine + half_n + d) % n

            @pl.when(o % half_n != seat)
            def _():
                narrow(o, (o // half_n + half) % 2, seat).start()

        loop(n, narrow_start)
        for kind in range(2):
            narrow_own(kind).start()
    for c in range(lead + 1, chunks):
        push(c, ())

    for a in range(lons // tile):
        table[:, a * tile : (a + 1) * tile] = (trig(a) * far[2, :, a : a + 1]).astype(jnp.bfloat16)
    give_table = pltpu.make_async_copy(table, synthesis, loc.at[4, 0])
    give_table.start()

    def take(source, bands):
        landed = pltpu.make_async_copy(source, got.at[pl.ds(0, bands * level_parts)], loc.at[4, 1])
        landed.start()
        landed.wait()

        def gather(q):
            at = pl.ds(pl.multiple_of(q * lats, lats), lats)
            for g in range(level_parts):
                wide[g] = got[q * level_parts + g].astype(jnp.float32).reshape(levels * pairs, lats)
                for k in range(pairs):
                    rows[k, pl.ds(g * levels, levels), at] = wide[g, pl.ds(k, levels, stride=pairs), :]

        loop(bands, gather)

    def spread(s, bands):
        for q in range(bands):
            for g in range(level_parts):
                for c in range(2):
                    split[q * level_parts + g, pl.ds(2 * s + c, levels, stride=pairs), :] = mix[
                        pl.ds(c * total + g * levels, levels), q * lats : (q + 1) * lats
                    ]

    def whole(c):
        others(lambda peer: forward(c, mine, peer, ()).wait_recv())
        forward_own(c, ()).wait()
        take(land.at[c], lat_parts)
        low = upper if cap and c < slots // 2 // GROUP else 0

        def slot(s):
            here = order[c * GROUP + s]
            legendre = basis_v[here, :, low:]
            columns = rows[pl.ds(2 * s, 2)].reshape(2 * total, lat_total).astype(jnp.bfloat16)
            coeffs = jnp.dot(columns, legendre, preferred_element_type=jnp.float32)
            mask = alive[c * GROUP + s][:, low:] > 0.5
            solved = []
            for k in range(2):
                part = coeffs[k * total : (k + 1) * total].astype(jnp.bfloat16)
                part = jnp.dot(solver_v[here], part, preferred_element_type=jnp.float32)
                solved.append(jnp.where(mask, part, 0.0))
            solved = jnp.concatenate(solved, axis=0).astype(jnp.bfloat16)
            mix[...] = lax.dot_general(
                solved, legendre, (((1,), (1,)), ((), ())), preferred_element_type=jnp.float32
            )
            spread(s, lat_parts)

        loop(GROUP, slot)
        others(lambda peer: forward(c, peer, mine, ()).wait_send())

        def fill(peer):
            buf[c, peer] = split[peer].astype(jnp.bfloat16).reshape(levels, pairs, lats)

        fill(mine)
        backward_own(c).start()

        def send(peer):
            fill(peer)
            backward(c, peer, mine).start()

        in_turn(send)

    def narrow_coeffs(kind, legendre):
        seats(lambda j: narrow(j, kind, j).wait_recv())
        narrow_own(kind).wait()
        take(land_t.at[kind], lat_parts // 2)
        acc[...] = jnp.zeros_like(acc)

        def one(w):
            columns = rows[pl.ds(2 * w, 2), :, :half_lats].reshape(2 * total, half_lats).astype(jnp.bfloat16)
            part = jnp.dot(columns, legendre(), preferred_element_type=jnp.float32)
            acc[...] = jnp.where(who[kind] == w, part, acc[...])

        loop(GROUP, one)

    def narrow_synthesis(kind, source, legendre):
        def one(w):
            solved = jnp.where(who[kind] == w, source[...].astype(jnp.float32), 0.0).astype(jnp.bfloat16)
            mix[:, :half_lats] = lax.dot_general(
                solved, legendre(), (((1,), (1,)), ((), ())), preferred_element_type=jnp.float32
            )
            spread(w, lat_parts // 2)

        loop(GROUP, one)

        def fill(j):
            buf[0, kind * half_n + j] = split[j].astype(jnp.bfloat16).reshape(levels, pairs, lats)

        owner = mine if kind == 0 else mirror
        fill(seat)
        narrow_back_own(kind).start()

        def send(j):
            fill(j)
            narrow_back(kind, j, owner).start()

        seats(send)

    if cap:
        give_part = remote(part_out, part_in, ms.at[1], mr.at[1], mirror)
        give_solved = remote(solved_out, solved_in, ms.at[2], mr.at[2], mirror)
        whole(1)
        give_rows.wait_recv()
        relay[...] = given[...]

        def pass_rows(d):
            return pltpu.make_async_remote_copy(
                src_ref=relay,
                dst_ref=passed.at[d - 1],
                send_sem=ms.at[2 + d],
                recv_sem=mr.at[2 + d],
                device_id=twin(d),
                device_id_type=pl.DeviceIdType.MESH,
            )

        def keep_rows(part, value):
            other[pl.ds(pl.multiple_of(part * share, share), share)] = value

        for d in range(1, members):
            pass_rows(d).start()
        keep_rows(member, given[...])
        for d in range(1, members):
            pass_rows(d).wait()
            keep_rows((member + members - d) % members, passed[d - 1])

        narrow_coeffs(1, lambda: other[...])
        part_out[...] = acc[...].astype(jnp.bfloat16)
        give_part.start()
        whole(2)
        narrow_coeffs(0, lambda: packed[near_rows])
        give_part.wait_recv()
        acc[...] += part_in[...].astype(jnp.float32)

        def solve(w):
            for k in range(2):
                at = pl.ds(k * total, total)
                part = jnp.dot(
                    solver_v[order[w]], acc[at].astype(jnp.bfloat16), preferred_element_type=jnp.float32
                )
                split_at = who[0] == w
                solved_f[at] = jnp.where(split_at, part, solved_f[at])

        solved_f[...] = jnp.zeros_like(solved_f)
        loop(GROUP, solve)
        solved_out[...] = solved_f[...].astype(jnp.bfloat16)
        give_solved.start()

        def narrow_sent(d):
            o = (mine + half_n + d) % n

            @pl.when(o % half_n != seat)
            def _():
                narrow(o, (o // half_n + half) % 2, seat).wait_send()

        loop(n, narrow_sent)
        narrow_synthesis(0, solved_out, lambda: packed[near_rows])
        for c in range(3, chunks):
            whole(c)
        give_solved.wait_recv()
        narrow_synthesis(1, solved_in, lambda: other[...])
        for copy in (give_rows, give_part, give_solved):
            copy.wait_send()
        for kind in range(2):
            owner = mine if kind == 0 else mirror
            narrow_back_own(kind).wait()
            seats(lambda j, kind=kind, owner=owner: narrow_back(kind, j, owner).wait_send())

            def arrived(j, kind=kind):
                narrow_back(kind, j, ((half + kind) % 2) * half_n + j).wait_recv()

            seats(arrived)
    else:
        for c in range(chunks):
            whole(c)
    for c in range(lead, chunks):
        others(lambda peer, c=c: backward(c, peer, mine).wait_send())
        others(lambda peer, c=c: backward(c, mine, peer).wait_recv())
        backward_own(c).wait()
    give_table.wait()


def fused(state, forcing, basis, solver, near, far, alive, order, key, who, n, level_parts, cap, number):
    levels, lats, lons = state.shape
    slots, lat_total, degrees = basis.shape
    total = solver.shape[1]
    pairs = 2 * GROUP
    chunks = slots // GROUP
    table_rows = near.shape[1]
    lanes = cap if cap else 128
    half_lats = lat_total // 2
    members = lax.axis_size("members")
    some = lambda *shape: shape if cap else (16, 128)
    message = (levels, pairs, lats)
    vmem = pl.BlockSpec(memory_space=pltpu.VMEM)
    hbm = pl.BlockSpec(memory_space=pl.ANY)
    smem = pl.BlockSpec(memory_space=pltpu.SMEM)
    short = (16, 16, 128)
    bf16, f32 = jnp.bfloat16, jnp.float32
    _, _, back, synthesis = pl.pallas_call(
        functools.partial(fused_kernel, n, level_parts, cap),
        out_shape=(
            jax.ShapeDtypeStruct((chunks, n, *message), bf16),
            jax.ShapeDtypeStruct((2, n // 2, *(message if cap else short)), bf16),
            jax.ShapeDtypeStruct((chunks, n, *message), bf16),
            jax.ShapeDtypeStruct((table_rows, lons), bf16),
        ),
        in_specs=[hbm, hbm, hbm, hbm, vmem, vmem, vmem, smem, vmem, vmem],
        out_specs=(hbm, hbm, hbm, hbm),
        scratch_shapes=[
            pltpu.VMEM((table_rows, lons), bf16),
            pltpu.VMEM((chunks, n, *message), bf16),
            pltpu.VMEM(basis.shape, bf16),
            pltpu.VMEM(solver.shape, bf16),
            pltpu.VMEM((n, *message), bf16),
            pltpu.VMEM((level_parts, levels * pairs, lats), f32),
            pltpu.VMEM((pairs, total, lat_total), f32),
            pltpu.VMEM((2 * total, lat_total), f32),
            pltpu.VMEM((n, levels * pairs, lats), f32),
            pltpu.VMEM((2, STEP, lats, lons), bf16),
            pltpu.VMEM((2, STEP, lats, lons), bf16),
            pltpu.VMEM(some(lat_total, lanes), bf16),
            pltpu.VMEM(some(half_lats // members, lanes), bf16),
            pltpu.VMEM(some(half_lats // members, lanes), bf16),
            pltpu.VMEM((max(members - 1, 1), *some(half_lats // members, lanes)), bf16),
            pltpu.VMEM(some(half_lats, lanes), bf16),
            pltpu.VMEM(some(2 * total, lanes), f32),
            pltpu.VMEM(some(2 * total, lanes), f32),
            pltpu.VMEM(some(2 * total, lanes), bf16),
            pltpu.VMEM(some(2 * total, lanes), bf16),
            pltpu.VMEM(some(2 * total, lanes), bf16),
            pltpu.VMEM(some(2 * total, lanes), bf16),
            pltpu.SemaphoreType.DMA((chunks, n)),
            pltpu.SemaphoreType.DMA((chunks, n)),
            pltpu.SemaphoreType.DMA((chunks, n)),
            pltpu.SemaphoreType.DMA((chunks, n)),
            pltpu.SemaphoreType.DMA((n,)),
            pltpu.SemaphoreType.DMA((2, n // 2)),
            pltpu.SemaphoreType.DMA((2 + members,)),
            pltpu.SemaphoreType.DMA((2 + members,)),
            pltpu.SemaphoreType.DMA((5, max(chunks, 2))),
            pltpu.SemaphoreType.DMA((3, 2)),
        ],
        compiler_params=pltpu.CompilerParams(
            collective_id=number, has_side_effects=True, vmem_limit_bytes=61 << 20
        ),
    )(state, forcing, basis, solver, near, far, alive, order, key, who)
    return back, synthesis

def small_tables(waves, lon_count, tile):
    waves = jnp.repeat(waves, 2)[:, None]
    quarter = (jnp.arange(waves.shape[0], dtype=jnp.int32) % 2)[:, None] * (lon_count // 4)
    unit = 2.0 * math.pi / lon_count
    fine = jnp.arange(tile, dtype=jnp.int32)[None, :] * waves % lon_count
    coarse = jnp.arange(lon_count // tile, dtype=jnp.int32)[None, :] * tile * waves + quarter
    fine, coarse = fine.astype(jnp.float32) * unit, (coarse % lon_count).astype(jnp.float32) * unit
    factor = 1.0 / math.sqrt(lon_count)
    weights = jnp.broadcast_to(jnp.where(waves == 0, 1.0, 2.0), coarse.shape)
    near = jnp.stack([jnp.cos(fine), jnp.sin(fine)])
    far = jnp.stack([jnp.cos(coarse) * factor, jnp.sin(coarse) * factor, weights])
    return near, far


def slot_order(waves, n):
    mine = waves.reshape(n, -1)
    slots = mine.shape[1]
    rank = jnp.sum((mine[:, None, :] > mine[:, :, None]).astype(jnp.int32), axis=2)
    here = rank[:, :, None] == jnp.arange(slots, dtype=jnp.int32)
    ranked = jnp.sum(jnp.where(here, mine[:, :, None], 0), axis=1)
    order = jnp.sum(jnp.where(here, jnp.arange(slots, dtype=jnp.int32)[None, :, None], 0), axis=1)
    return ranked, order


def packing(ranked, degrees, lanes):
    first = ranked[:, :GROUP]
    counts = degrees - first
    before = jnp.arange(GROUP)[:, None] > jnp.arange(GROUP)[None, :]
    starts = jnp.sum(jnp.where(before, counts[:, None, :], 0), axis=2)
    lane = jnp.arange(lanes, dtype=jnp.int32)
    inside = (lane >= starts[:, :, None]) & (lane < (starts + counts)[:, :, None])
    upper = degrees // 2
    wave = jnp.arange(GROUP, dtype=jnp.int32)[None, :, None]
    column = wave * upper + first[:, :, None] - upper + lane - starts[:, :, None]
    key = jnp.sum(jnp.where(inside, column + 1, 0), axis=1) - 1
    who = jnp.sum(jnp.where(inside, wave + 1, 0), axis=1) - 1
    return key, who


def fast(state, forcing, basis, solver, waves, lat_parts, level_parts):
    levels, lats, lons = state.shape
    slots, _, degrees = basis.shape
    n = lat_parts * level_parts
    chunks = slots // GROUP
    owner = lax.axis_index(OWNERS)

    mirror = (owner + n // 2) % n
    ranked, order = slot_order(waves, n)
    flat = ranked.reshape(n, chunks, GROUP).transpose(1, 0, 2).reshape(-1)
    near, far = small_tables(flat, lons, 128)
    mine = lax.dynamic_index_in_dim(ranked, owner, 0, keepdims=False)
    live = jnp.arange(degrees, dtype=jnp.int32)[None, :] >= mine[:, None]
    alive = live.astype(jnp.float32)[:, None, :]
    order = lax.dynamic_index_in_dim(order, owner, 0, keepdims=False)

    def branch(number):
        cap = CAPS[number]

        def run(operands):
            both = jnp.stack(
                [lax.dynamic_index_in_dim(ranked, o, 0, keepdims=False) for o in (owner, mirror)]
            )
            key, who = packing(both, degrees, max(cap, 128))
            return fused(*operands, key[:1], who[:, None], n, level_parts, cap, number)

        return run

    needed = jnp.max(jnp.sum(degrees - ranked[:, :GROUP], axis=1))
    unfit = sum((needed > cap).astype(jnp.int32) for cap in CAPS if cap)
    back, synthesis = lax.switch(
        unfit,
        [branch(number) for number in range(len(CAPS))],
        (state, forcing, basis, solver, near, far, alive, order),
    )
    synthesis = synthesis.reshape(chunks, n, 2 * GROUP, lons)
    result = jnp.einsum("holkx,hokj->lxj", back, synthesis, preferred_element_type=jnp.float32)
    return result.astype(jnp.bfloat16)


def make_shards(lat_parts, level_parts):
    owners = lat_parts * level_parts

    def shards(state, forcing, basis, solver, waves):
        levels, lats, lons = state.shape
        slots, lat_total, degrees = basis.shape
        level_total = solver.shape[1]
        owner = lax.axis_index(OWNERS)
        my_waves = lax.dynamic_slice_in_dim(waves, owner * slots, slots)
        live = jnp.arange(degrees, dtype=jnp.int32)[None, :] >= my_waves[:, None]
        if (
            lats % 128 == 0
            and lons % 512 == 0
            and slots % (4 * GROUP) == 0
            and levels % STEP == 0
            and lat_parts % 2 == 0
        ):
            return fast(state, forcing, basis, solver, waves, lat_parts, level_parts)
        present = state.astype(jnp.float32)
        explicit = (
            present
            + 0.5 * forcing.astype(jnp.float32)
            - 0.3 * present * present * present / (1.0 + present * present)
        ).astype(jnp.bfloat16)
        raw = raw_table(waves, lons)
        analysis = raw.astype(jnp.bfloat16)
        weights = jnp.where(waves == 0, 1.0, 2.0).astype(jnp.float32)
        synthesis = (raw * weights[:, None, None]).astype(jnp.bfloat16)
        chunks = CHUNKS
        part = slots // chunks
        analysis = analysis.reshape(owners, slots, 2, lons)
        synthesis = synthesis.reshape(owners, slots, 2, lons)
        sent = []
        for i in range(chunks):
            own = slice(i * part, (i + 1) * part)
            spectral = jnp.einsum(
                "oscj,lxj->osclx", analysis[:, own], explicit, preferred_element_type=jnp.float32
            ).astype(jnp.bfloat16)
            sent.append(lax.all_to_all(spectral, OWNERS, split_axis=0, concat_axis=0, tiled=True))
        back = []
        for i in range(chunks):
            own = slice(i * part, (i + 1) * part)
            got = sent[i].reshape(lat_parts, level_parts, part, 2, levels, lats)
            table = basis[own]
            columns = got.transpose(2, 3, 1, 4, 0, 5).reshape(part, 2 * level_total, lat_total)
            coeffs = jnp.einsum(
                "srx,sxn->srn", columns, table, preferred_element_type=jnp.float32
            ).astype(jnp.bfloat16).reshape(part, 2, level_total, degrees)
            solved = jnp.einsum(
                "skl,scln->sckn", solver[own], coeffs, preferred_element_type=jnp.float32
            )
            solved = jnp.where(live[own][:, None, None, :], solved, 0.0).astype(jnp.bfloat16)
            grid = jnp.einsum(
                "srn,sxn->srx",
                solved.reshape(part, 2 * level_total, degrees),
                table,
                preferred_element_type=jnp.float32,
            ).astype(jnp.bfloat16)
            grid = grid.reshape(part, 2, level_parts, levels, lat_parts, lats)
            grid = grid.transpose(4, 2, 0, 1, 3, 5).reshape(owners, part, 2, levels, lats)
            back.append(lax.all_to_all(grid, OWNERS, split_axis=0, concat_axis=0, tiled=True))
        waved = jnp.concatenate(back, axis=1)
        result = jnp.einsum(
            "osclx,oscj->lxj", waved, synthesis, preferred_element_type=jnp.float32
        )
        return result.astype(jnp.bfloat16)

    return shards


def solution(mesh):
    lat_parts = mesh.shape["lat"]
    level_parts = mesh.shape["lev"] * mesh.shape["sub"]
    return jax.shard_map(
        make_shards(lat_parts, level_parts),
        mesh=mesh,
        in_specs=(
            P(("members", "lev", "sub"), "lat", None),
            P(("members", "lev", "sub"), "lat", None),
            P(OWNERS, None, None),
            P(OWNERS, None, None),
            P(),
        ),
        out_specs=P(("members", "lev", "sub"), "lat", None),
        check_vma=False,
    )
```

```python
import functools
import math

import jax
import jax.numpy as jnp
from jax import lax
from jax.experimental import pallas as pl
from jax.experimental.pallas import tpu as pltpu
from jax.sharding import PartitionSpec as P

CHUNKS = 4
GROUP = 8
STEP = 2
CAPS = (896, 0)
OWNERS = ("lat", "lev", "sub")


def raw_table(waves, lon_count):
    meridian = jnp.arange(lon_count, dtype=jnp.int32)
    phases = waves[:, None] * meridian[None, :] % lon_count
    angles = phases.astype(jnp.float32) * (2.0 * math.pi / lon_count)
    factor = 1.0 / math.sqrt(lon_count)
    return jnp.stack([jnp.cos(angles), -jnp.sin(angles)], axis=1) * factor


def place(peer, level_parts):
    subs = lax.axis_size("sub")
    return {
        "lat": peer // level_parts,
        "lev": (peer % level_parts) // subs,
        "sub": peer % subs,
    }


def my_place(level_parts):
    subs = lax.axis_size("sub")
    return lax.axis_index("lat") * level_parts + lax.axis_index("lev") * subs + lax.axis_index("sub")


def fused_kernel(
    n, level_parts, cap,
    state, forcing, basis, solver, near, far, alive, order, key, who,
    land, land_t, back, synthesis,
    table, buf, low_v, high_v, solver_v, got, wide, rows, mix, split, st, fo,
    packed, given, passed, other, acc, solved_f, part_out, part_in, solved_out, solved_in,
    fs, fr, bs, br, ts, tr, ms, mr, hs, hr, loc, ins,
):
    levels, lats, lons = state.shape
    chunks, _, _, pairs, _ = buf.shape
    slots, lat_total, degrees = basis.shape
    total = levels * level_parts
    lat_parts = n // level_parts
    steps = levels // STEP
    tile = near.shape[2]
    mine = my_place(level_parts)
    lat, group, sub = mine // level_parts, mine % level_parts, lax.axis_index("sub")
    half_n = n // 2
    half, seat = mine // half_n, mine % half_n
    mirror = (mine + half_n) % n
    member, members = lax.axis_index("members"), lax.axis_size("members")
    half_lats = lat_total // 2
    upper = degrees // 2

    def remote(src, dst, send_sem, recv_sem, peer):
        return pltpu.make_async_remote_copy(
            src_ref=src,
            dst_ref=dst,
            send_sem=send_sem,
            recv_sem=recv_sem,
            device_id=place(peer, level_parts),
            device_id_type=pl.DeviceIdType.MESH,
        )

    def loop(count, body):
        def run(i, carry):
            body(i)
            return carry

        lax.fori_loop(0, count, run, 0)

    def forward(c, peer, landing, cut):
        return remote(
            buf.at[(c, peer, *cut)], land.at[(c, landing, *cut)], fs.at[c, peer], fr.at[c, landing], peer
        )

    def forward_own(c, cut):
        return pltpu.make_async_copy(buf.at[(c, mine, *cut)], land.at[(c, mine, *cut)], loc.at[0, c])

    def backward(c, peer, landing):
        return remote(buf.at[c, peer], back.at[c, landing], bs.at[c, peer], br.at[c, landing], peer)

    def backward_own(c):
        return pltpu.make_async_copy(buf.at[c, mine], back.at[c, mine], loc.at[1, c])

    def in_turn(start):
        def one(t):
            turn = (lat + t // level_parts + (1 - sub) * (lat_parts // 2)) % lat_parts
            peer = turn * level_parts + (group + t) % level_parts

            @pl.when(peer != mine)
            def _():
                start(peer)

        loop(n, one)

    def others(wait):
        loop(n - 1, lambda d: wait((mine + 1 + d) % n))

    def push(c, cut):
        in_turn(lambda peer: forward(c, peer, mine, cut).start())
        forward_own(c, cut).start()

    def narrow(o, kind, place_in):
        return remote(
            buf.at[0, o], land_t.at[kind, place_in], ts.at[o], tr.at[kind, place_in], half * half_n + o % half_n
        )

    def narrow_own(kind):
        owner = ((half + kind) % 2) * half_n + seat
        return pltpu.make_async_copy(buf.at[0, owner], land_t.at[kind, seat], loc.at[2, kind])

    def narrow_back(kind, to, owner):
        return remote(
            buf.at[0, kind * half_n + to], back.at[0, owner], bs.at[0, kind * half_n + to], br.at[0, owner],
            half * half_n + to,
        )

    def narrow_back_own(kind):
        owner = ((half + kind) % 2) * half_n + seat
        return pltpu.make_async_copy(buf.at[0, kind * half_n + seat], back.at[0, owner], loc.at[3, kind])

    def seats(do):
        def one(d):
            do((seat + 1 + d) % half_n)

        loop(half_n - 1, one)

    def trig(a):
        return far[0, :, a : a + 1] * near[0] - far[1, :, a : a + 1] * near[1]

    def fetch(i):
        slot = i % 2
        cut = pl.ds(i * STEP, STEP)
        return (
            pltpu.make_async_copy(state.at[cut], st.at[slot], ins.at[0, slot]),
            pltpu.make_async_copy(forcing.at[cut], fo.at[slot], ins.at[1, slot]),
        )

    sibling = mine + 1 - 2 * sub
    high_part = basis.at[:, :, pl.ds(upper, upper)]
    first, second = pl.ds(0, slots), pl.ds(slots, slots)
    weights = (
        pltpu.make_async_copy(basis.at[:, :, pl.ds(0, upper)], low_v, ins.at[2, 0]),
        pltpu.make_async_copy(high_part, high_v.at[first], ins.at[3, 0]),
        pltpu.make_async_copy(solver, solver_v.at[first], ins.at[2, 1]),
        remote(high_part, high_v.at[second], hs.at[0], hr.at[0], sibling),
        remote(solver, solver_v.at[second], hs.at[1], hr.at[1], sibling),
    )

    for copy in fetch(0):
        copy.start()
    barrier = pltpu.get_barrier_semaphore()
    others(
        lambda peer: pl.semaphore_signal(
            barrier, inc=1, device_id=place(peer, level_parts), device_id_type=pl.DeviceIdType.MESH
        )
    )
    def twin(d):
        return dict(place(mine, level_parts), members=(member + d) % members)

    if cap:
        for d in range(1, members):
            pl.semaphore_signal(
                barrier, inc=1, device_id=twin(d), device_id_type=pl.DeviceIdType.MESH
            )
    greeted = n - 1 + (members - 1 if cap else 0)
    for a in range(lons // tile):
        table[:, a * tile : (a + 1) * tile] = trig(a).astype(jnp.bfloat16)

    lead = 1 if cap else 0

    def dft(i):
        for copy in fetch(i):
            copy.wait()

        @pl.when(i + 1 < steps)
        def _():
            for copy in fetch(i + 1):
                copy.start()

        slot = i % 2
        present = st[slot].astype(jnp.float32)
        explicit = (
            present
            + 0.5 * fo[slot].astype(jnp.float32)
            - 0.3 * present * present * present / (1.0 + present * present)
        ).astype(jnp.bfloat16)
        spectral = lax.dot_general(
            table[...],
            explicit.reshape(STEP * lats, lons),
            (((1,), (1,)), ((), ())),
            preferred_element_type=jnp.float32,
        ).astype(jnp.bfloat16)
        spectral = spectral.reshape(chunks, n, pairs, STEP * lats)
        for level in range(STEP):
            buf[:, :, i * STEP + level] = spectral[..., level * lats : (level + 1) * lats]

        @pl.when(i == 0)
        def _():
            pl.semaphore_wait(barrier, greeted)
            for copy in weights:
                copy.start()

        push(lead, (pl.ds(i * STEP, STEP),))

    loop(steps, dft)
    for copy in weights:
        copy.wait()

    if cap:
        lanes = packed.shape[1]
        place_of = lax.broadcasted_iota(jnp.int32, (upper, lanes), 0)
        packed[...] = jnp.zeros_like(packed)

        def pack(w):
            pick = (place_of + w * upper == key[...]).astype(jnp.float32).astype(jnp.bfloat16)
            part = jnp.dot(
                high_v[order[w]], pick, preferred_element_type=jnp.float32
            )
            packed[...] = (packed[...].astype(jnp.float32) + part).astype(jnp.bfloat16)

        loop(GROUP, pack)
        share = half_lats // members
        far_share = pl.ds(pl.multiple_of((1 - half) * half_lats + member * share, share), share)
        near_rows = pl.ds(pl.multiple_of(half * half_lats, half_lats), half_lats)
        give_rows = remote(packed.at[far_share], given, ms.at[0], mr.at[0], mirror)
        give_rows.start()

        def narrow_start(d):
            o = (mine + half_n + d) % n

            @pl.when(o % half_n != seat)
            def _():
                narrow(o, (o // half_n + half) % 2, seat).start()

        loop(n, narrow_start)
        for kind in range(2):
            narrow_own(kind).start()
    for c in range(lead + 1, chunks):
        push(c, ())

    for a in range(lons // tile):
        table[:, a * tile : (a + 1) * tile] = (trig(a) * far[2, :, a : a + 1]).astype(jnp.bfloat16)
    give_table = pltpu.make_async_copy(table, synthesis, loc.at[4, 0])
    give_table.start()

    def take(source, bands):
        landed = pltpu.make_async_copy(source, got.at[pl.ds(0, bands * level_parts)], loc.at[4, 1])
        landed.start()
        landed.wait()

        def gather(q):
            at = pl.ds(pl.multiple_of(q * lats, lats), lats)
            for g in range(level_parts):
                wide[g] = got[q * level_parts + g].astype(jnp.float32).reshape(levels * pairs, lats)
                for k in range(pairs):
                    rows[k, pl.ds(g * levels, levels), at] = wide[g, pl.ds(k, levels, stride=pairs), :]

        loop(bands, gather)

    def spread(s, bands):
        for q in range(bands):
            for g in range(level_parts):
                for c in range(2):
                    split[q * level_parts + g, pl.ds(2 * s + c, levels, stride=pairs), :] = mix[
                        pl.ds(c * total + g * levels, levels), q * lats : (q + 1) * lats
                    ]

    def whole(c):
        others(lambda peer: forward(c, mine, peer, ()).wait_recv())
        forward_own(c, ()).wait()
        take(land.at[c], lat_parts)
        low = upper if c < slots // 2 // GROUP else 0

        def slot(s):
            here = order[c * GROUP + s]
            legendre = high_v[here]
            if not low:
                legendre = jnp.concatenate([low_v[here], legendre], axis=1)
            columns = rows[pl.ds(2 * s, 2)].reshape(2 * total, lat_total).astype(jnp.bfloat16)
            coeffs = jnp.dot(columns, legendre, preferred_element_type=jnp.float32)
            mask = alive[c * GROUP + s][:, low:] > 0.5
            solved = []
            for k in range(2):
                part = coeffs[k * total : (k + 1) * total].astype(jnp.bfloat16)
                part = jnp.dot(solver_v[here], part, preferred_element_type=jnp.float32)
                solved.append(jnp.where(mask, part, 0.0))
            solved = jnp.concatenate(solved, axis=0).astype(jnp.bfloat16)
            mix[...] = lax.dot_general(
                solved, legendre, (((1,), (1,)), ((), ())), preferred_element_type=jnp.float32
            )
            spread(s, lat_parts)

        loop(GROUP, slot)
        others(lambda peer: forward(c, peer, mine, ()).wait_send())

        def fill(peer):
            buf[c, peer] = split[peer].astype(jnp.bfloat16).reshape(levels, pairs, lats)

        fill(mine)
        backward_own(c).start()

        def send(peer):
            fill(peer)
            backward(c, peer, mine).start()

        in_turn(send)

    def narrow_coeffs(kind, legendre):
        seats(lambda j: narrow(j, kind, j).wait_recv())
        narrow_own(kind).wait()
        take(land_t.at[kind], lat_parts // 2)
        acc[...] = jnp.zeros_like(acc)

        def one(w):
            columns = rows[pl.ds(2 * w, 2), :, :half_lats].reshape(2 * total, half_lats).astype(jnp.bfloat16)
            part = jnp.dot(columns, legendre(), preferred_element_type=jnp.float32)
            acc[...] = jnp.where(who[kind] == w, part, acc[...])

        loop(GROUP, one)

    def narrow_synthesis(kind, source, legendre):
        def one(w):
            solved = jnp.where(who[kind] == w, source[...].astype(jnp.float32), 0.0).astype(jnp.bfloat16)
            mix[:, :half_lats] = lax.dot_general(
                solved, legendre(), (((1,), (1,)), ((), ())), preferred_element_type=jnp.float32
            )
            spread(w, lat_parts // 2)

        loop(GROUP, one)

        def fill(j):
            buf[0, kind * half_n + j] = split[j].astype(jnp.bfloat16).reshape(levels, pairs, lats)

        owner = mine if kind == 0 else mirror
        fill(seat)
        narrow_back_own(kind).start()

        def send(j):
            fill(j)
            narrow_back(kind, j, owner).start()

        seats(send)

    if cap:
        give_part = remote(part_out, part_in, ms.at[1], mr.at[1], mirror)
        give_solved = remote(solved_out, solved_in, ms.at[2], mr.at[2], mirror)
        whole(1)
        give_rows.wait_recv()

        def pass_rows(d):
            return pltpu.make_async_remote_copy(
                src_ref=given,
                dst_ref=passed.at[d - 1],
                send_sem=ms.at[2 + d],
                recv_sem=mr.at[2 + d],
                device_id=twin(d),
                device_id_type=pl.DeviceIdType.MESH,
            )

        def keep_rows(part, value):
            other[pl.ds(pl.multiple_of(part * share, share), share)] = value

        for d in range(1, members):
            pass_rows(d).start()
        keep_rows(member, given[...])
        for d in range(1, members):
            pass_rows(d).wait()
            keep_rows((member + members - d) % members, passed[d - 1])

        narrow_coeffs(1, lambda: other[...])
        part_out[...] = acc[...].astype(jnp.bfloat16)
        give_part.start()
        whole(2)
        narrow_coeffs(0, lambda: packed[near_rows])
        give_part.wait_recv()
        acc[...] += part_in[...].astype(jnp.float32)

        def solve(w):
            for k in range(2):
                at = pl.ds(k * total, total)
                part = jnp.dot(
                    solver_v[order[w]], acc[at].astype(jnp.bfloat16), preferred_element_type=jnp.float32
                )
                split_at = who[0] == w
                solved_f[at] = jnp.where(split_at, part, solved_f[at])

        solved_f[...] = jnp.zeros_like(solved_f)
        loop(GROUP, solve)
        solved_out[...] = solved_f[...].astype(jnp.bfloat16)
        give_solved.start()

        def narrow_sent(d):
            o = (mine + half_n + d) % n

            @pl.when(o % half_n != seat)
            def _():
                narrow(o, (o // half_n + half) % 2, seat).wait_send()

        loop(n, narrow_sent)
        narrow_synthesis(0, solved_out, lambda: packed[near_rows])
        for c in range(3, chunks):
            whole(c)
        give_solved.wait_recv()
        narrow_synthesis(1, solved_in, lambda: other[...])
        for copy in (give_rows, give_part, give_solved):
            copy.wait_send()
        for kind in range(2):
            owner = mine if kind == 0 else mirror
            narrow_back_own(kind).wait()
            seats(lambda j, kind=kind, owner=owner: narrow_back(kind, j, owner).wait_send())

            def arrived(j, kind=kind):
                narrow_back(kind, j, ((half + kind) % 2) * half_n + j).wait_recv()

            seats(arrived)
    else:
        for c in range(chunks):
            whole(c)
    for c in range(lead, chunks):
        others(lambda peer, c=c: backward(c, peer, mine).wait_send())
        others(lambda peer, c=c: backward(c, mine, peer).wait_recv())
        backward_own(c).wait()
    give_table.wait()


def fused(state, forcing, basis, solver, near, far, alive, order, key, who, n, level_parts, cap, number):
    levels, lats, lons = state.shape
    slots, lat_total, degrees = basis.shape
    total = solver.shape[1]
    pairs = 2 * GROUP
    chunks = slots // GROUP
    table_rows = near.shape[1]
    lanes = cap if cap else 128
    half_lats = lat_total // 2
    members = lax.axis_size("members")
    some = lambda *shape: shape if cap else (16, 128)
    message = (levels, pairs, lats)
    vmem = pl.BlockSpec(memory_space=pltpu.VMEM)
    hbm = pl.BlockSpec(memory_space=pl.ANY)
    smem = pl.BlockSpec(memory_space=pltpu.SMEM)
    short = (16, 16, 128)
    bf16, f32 = jnp.bfloat16, jnp.float32
    _, _, back, synthesis = pl.pallas_call(
        functools.partial(fused_kernel, n, level_parts, cap),
        out_shape=(
            jax.ShapeDtypeStruct((chunks, n, *message), bf16),
            jax.ShapeDtypeStruct((2, n // 2, *(message if cap else short)), bf16),
            jax.ShapeDtypeStruct((chunks, n, *message), bf16),
            jax.ShapeDtypeStruct((table_rows, lons), bf16),
        ),
        in_specs=[hbm, hbm, hbm, hbm, vmem, vmem, vmem, smem, vmem, vmem],
        out_specs=(hbm, hbm, hbm, hbm),
        scratch_shapes=[
            pltpu.VMEM((table_rows, lons), bf16),
            pltpu.VMEM((chunks, n, *message), bf16),
            pltpu.VMEM((slots, lat_total, degrees // 2), bf16),
            pltpu.VMEM((2 * slots, lat_total, degrees // 2), bf16),
            pltpu.VMEM((2 * slots, total, total), bf16),
            pltpu.VMEM((n, *message), bf16),
            pltpu.VMEM((level_parts, levels * pairs, lats), f32),
            pltpu.VMEM((pairs, total, lat_total), f32),
            pltpu.VMEM((2 * total, lat_total), f32),
            pltpu.VMEM((n, levels * pairs, lats), f32),
            pltpu.VMEM((2, STEP, lats, lons), bf16),
            pltpu.VMEM((2, STEP, lats, lons), bf16),
            pltpu.VMEM(some(lat_total, lanes), bf16),
            pltpu.VMEM(some(half_lats // members, lanes), bf16),
            pltpu.VMEM((max(members - 1, 1), *some(half_lats // members, lanes)), bf16),
            pltpu.VMEM(some(half_lats, lanes), bf16),
            pltpu.VMEM(some(2 * total, lanes), f32),
            pltpu.VMEM(some(2 * total, lanes), f32),
            pltpu.VMEM(some(2 * total, lanes), bf16),
            pltpu.VMEM(some(2 * total, lanes), bf16),
            pltpu.VMEM(some(2 * total, lanes), bf16),
            pltpu.VMEM(some(2 * total, lanes), bf16),
            pltpu.SemaphoreType.DMA((chunks, n)),
            pltpu.SemaphoreType.DMA((chunks, n)),
            pltpu.SemaphoreType.DMA((chunks, n)),
            pltpu.SemaphoreType.DMA((chunks, n)),
            pltpu.SemaphoreType.DMA((n,)),
            pltpu.SemaphoreType.DMA((2, n // 2)),
            pltpu.SemaphoreType.DMA((2 + members,)),
            pltpu.SemaphoreType.DMA((2 + members,)),
            pltpu.SemaphoreType.DMA((2,)),
            pltpu.SemaphoreType.DMA((2,)),
            pltpu.SemaphoreType.DMA((5, max(chunks, 2))),
            pltpu.SemaphoreType.DMA((4, 2)),
        ],
        compiler_params=pltpu.CompilerParams(
            collective_id=number, has_side_effects=True, vmem_limit_bytes=63 << 20
        ),
    )(state, forcing, basis, solver, near, far, alive, order, key, who)
    return back, synthesis

def small_tables(waves, lon_count, tile):
    waves = jnp.repeat(waves, 2)[:, None]
    quarter = (jnp.arange(waves.shape[0], dtype=jnp.int32) % 2)[:, None] * (lon_count // 4)
    unit = 2.0 * math.pi / lon_count
    fine = jnp.arange(tile, dtype=jnp.int32)[None, :] * waves % lon_count
    coarse = jnp.arange(lon_count // tile, dtype=jnp.int32)[None, :] * tile * waves + quarter
    fine, coarse = fine.astype(jnp.float32) * unit, (coarse % lon_count).astype(jnp.float32) * unit
    factor = 1.0 / math.sqrt(lon_count)
    weights = jnp.broadcast_to(jnp.where(waves == 0, 1.0, 2.0), coarse.shape)
    near = jnp.stack([jnp.cos(fine), jnp.sin(fine)])
    far = jnp.stack([jnp.cos(coarse) * factor, jnp.sin(coarse) * factor, weights])
    return near, far


def falling(values):
    return jnp.sum((values[:, None, :] > values[:, :, None]).astype(jnp.int32), axis=2)


def slot_order(waves, n):
    chips = waves.reshape(n // 2, -1)
    both = chips.shape[1]
    slots = both // 2
    rank = falling(chips)
    own = falling(waves.reshape(n, slots)).reshape(n // 2, both)
    source = jnp.arange(both, dtype=jnp.int32)
    core = (rank + 1) // 2 % 2
    to = jnp.where(rank < slots, core * slots + rank // 2, source // slots * slots + own)
    here = to[:, :, None] == source
    ranked = jnp.sum(jnp.where(here, chips[:, :, None], 0), axis=1).reshape(n, slots)
    order = jnp.sum(jnp.where(here, source[None, :, None], 0), axis=1).reshape(n // 2, 2, slots)
    order = (order + jnp.arange(2, dtype=jnp.int32)[:, None] * slots) % both
    return ranked, order.reshape(n, slots)


def packing(ranked, degrees, lanes):
    first = ranked[:, :GROUP]
    counts = degrees - first
    before = jnp.arange(GROUP)[:, None] > jnp.arange(GROUP)[None, :]
    starts = jnp.sum(jnp.where(before, counts[:, None, :], 0), axis=2)
    lane = jnp.arange(lanes, dtype=jnp.int32)
    inside = (lane >= starts[:, :, None]) & (lane < (starts + counts)[:, :, None])
    upper = degrees // 2
    wave = jnp.arange(GROUP, dtype=jnp.int32)[None, :, None]
    column = wave * upper + first[:, :, None] - upper + lane - starts[:, :, None]
    key = jnp.sum(jnp.where(inside, column + 1, 0), axis=1) - 1
    who = jnp.sum(jnp.where(inside, wave + 1, 0), axis=1) - 1
    return key, who


def fast(state, forcing, basis, solver, waves, lat_parts, level_parts):
    levels, lats, lons = state.shape
    slots, _, degrees = basis.shape
    n = lat_parts * level_parts
    chunks = slots // GROUP
    owner = lax.axis_index(OWNERS)

    mirror = (owner + n // 2) % n
    ranked, order = slot_order(waves, n)
    flat = ranked.reshape(n, chunks, GROUP).transpose(1, 0, 2).reshape(-1)
    near, far = small_tables(flat, lons, 128)
    mine = lax.dynamic_index_in_dim(ranked, owner, 0, keepdims=False)
    live = jnp.arange(degrees, dtype=jnp.int32)[None, :] >= mine[:, None]
    alive = live.astype(jnp.float32)[:, None, :]
    order = lax.dynamic_index_in_dim(order, owner, 0, keepdims=False)

    def branch(number):
        cap = CAPS[number]

        def run(operands):
            both = jnp.stack(
                [lax.dynamic_index_in_dim(ranked, o, 0, keepdims=False) for o in (owner, mirror)]
            )
            key, who = packing(both, degrees, max(cap, 128))
            return fused(*operands, key[:1], who[:, None], n, level_parts, cap, number)

        return run

    needed = jnp.max(jnp.sum(degrees - ranked[:, :GROUP], axis=1))
    unfit = sum((needed > cap).astype(jnp.int32) for cap in CAPS if cap)
    back, synthesis = lax.switch(
        unfit,
        [branch(number) for number in range(len(CAPS))],
        (state, forcing, basis, solver, near, far, alive, order),
    )
    synthesis = synthesis.reshape(chunks, n, 2 * GROUP, lons)
    result = jnp.einsum("holkx,hokj->lxj", back, synthesis, preferred_element_type=jnp.float32)
    return result.astype(jnp.bfloat16)


def make_shards(lat_parts, level_parts):
    owners = lat_parts * level_parts

    def shards(state, forcing, basis, solver, waves):
        levels, lats, lons = state.shape
        slots, lat_total, degrees = basis.shape
        level_total = solver.shape[1]
        owner = lax.axis_index(OWNERS)
        my_waves = lax.dynamic_slice_in_dim(waves, owner * slots, slots)
        live = jnp.arange(degrees, dtype=jnp.int32)[None, :] >= my_waves[:, None]
        if (
            lats % 128 == 0
            and lons % 512 == 0
            and slots == 4 * GROUP
            and lax.axis_size("sub") == 2
            and levels % STEP == 0
            and lat_parts % 2 == 0
        ):
            return fast(state, forcing, basis, solver, waves, lat_parts, level_parts)
        present = state.astype(jnp.float32)
        explicit = (
            present
            + 0.5 * forcing.astype(jnp.float32)
            - 0.3 * present * present * present / (1.0 + present * present)
        ).astype(jnp.bfloat16)
        raw = raw_table(waves, lons)
        analysis = raw.astype(jnp.bfloat16)
        weights = jnp.where(waves == 0, 1.0, 2.0).astype(jnp.float32)
        synthesis = (raw * weights[:, None, None]).astype(jnp.bfloat16)
        chunks = CHUNKS
        part = slots // chunks
        analysis = analysis.reshape(owners, slots, 2, lons)
        synthesis = synthesis.reshape(owners, slots, 2, lons)
        sent = []
        for i in range(chunks):
            own = slice(i * part, (i + 1) * part)
            spectral = jnp.einsum(
                "oscj,lxj->osclx", analysis[:, own], explicit, preferred_element_type=jnp.float32
            ).astype(jnp.bfloat16)
            sent.append(lax.all_to_all(spectral, OWNERS, split_axis=0, concat_axis=0, tiled=True))
        back = []
        for i in range(chunks):
            own = slice(i * part, (i + 1) * part)
            got = sent[i].reshape(lat_parts, level_parts, part, 2, levels, lats)
            table = basis[own]
            columns = got.transpose(2, 3, 1, 4, 0, 5).reshape(part, 2 * level_total, lat_total)
            coeffs = jnp.einsum(
                "srx,sxn->srn", columns, table, preferred_element_type=jnp.float32
            ).astype(jnp.bfloat16).reshape(part, 2, level_total, degrees)
            solved = jnp.einsum(
                "skl,scln->sckn", solver[own], coeffs, preferred_element_type=jnp.float32
            )
            solved = jnp.where(live[own][:, None, None, :], solved, 0.0).astype(jnp.bfloat16)
            grid = jnp.einsum(
                "srn,sxn->srx",
                solved.reshape(part, 2 * level_total, degrees),
                table,
                preferred_element_type=jnp.float32,
            ).astype(jnp.bfloat16)
            grid = grid.reshape(part, 2, level_parts, levels, lat_parts, lats)
            grid = grid.transpose(4, 2, 0, 1, 3, 5).reshape(owners, part, 2, levels, lats)
            back.append(lax.all_to_all(grid, OWNERS, split_axis=0, concat_axis=0, tiled=True))
        waved = jnp.concatenate(back, axis=1)
        result = jnp.einsum(
            "osclx,oscj->lxj", waved, synthesis, preferred_element_type=jnp.float32
        )
        return result.astype(jnp.bfloat16)

    return shards


def solution(mesh):
    lat_parts = mesh.shape["lat"]
    level_parts = mesh.shape["lev"] * mesh.shape["sub"]
    return jax.shard_map(
        make_shards(lat_parts, level_parts),
        mesh=mesh,
        in_specs=(
            P(("members", "lev", "sub"), "lat", None),
            P(("members", "lev", "sub"), "lat", None),
            P(OWNERS, None, None),
            P(OWNERS, None, None),
            P(),
        ),
        out_specs=P(("members", "lev", "sub"), "lat", None),
        check_vma=False,
    )
```

```python
import functools
import math

import jax
import jax.numpy as jnp
from jax import lax
from jax.experimental import pallas as pl
from jax.experimental.pallas import tpu as pltpu
from jax.sharding import PartitionSpec as P

CHUNKS = 4
GROUP = 8
STEP = 2
CAPS = (896, 0)
OWNERS = ("lat", "lev", "sub")


def raw_table(waves, lon_count):
    meridian = jnp.arange(lon_count, dtype=jnp.int32)
    phases = waves[:, None] * meridian[None, :] % lon_count
    angles = phases.astype(jnp.float32) * (2.0 * math.pi / lon_count)
    factor = 1.0 / math.sqrt(lon_count)
    return jnp.stack([jnp.cos(angles), -jnp.sin(angles)], axis=1) * factor


def place(peer, level_parts):
    subs = lax.axis_size("sub")
    return {
        "lat": peer // level_parts,
        "lev": (peer % level_parts) // subs,
        "sub": peer % subs,
    }


def my_place(level_parts):
    subs = lax.axis_size("sub")
    return lax.axis_index("lat") * level_parts + lax.axis_index("lev") * subs + lax.axis_index("sub")


def fused_kernel(
    n, level_parts, cap,
    state, forcing, basis, solver, cosine, sine, far, alive, order, key, who,
    land, land_t, back, synthesis,
    table, buf, low_v, high_v, solver_v, got, wide, rows, mix, split, st, fo,
    packed, given, passed, other, acc, solved_f, part_out, part_in, solved_out, solved_in,
    fs, fr, bs, br, ts, tr, ms, mr, hs, hr, loc, ins,
):
    levels, lats, lons = state.shape
    chunks, _, _, pairs, _ = buf.shape
    slots, lat_total, degrees = basis.shape
    total = levels * level_parts
    lat_parts = n // level_parts
    steps = levels // STEP
    tile = cosine.shape[1]
    mine = my_place(level_parts)
    lat, group, sub = mine // level_parts, mine % level_parts, lax.axis_index("sub")
    half_n = n // 2
    half, seat = mine // half_n, mine % half_n
    mirror = (mine + half_n) % n
    member, members = lax.axis_index("members"), lax.axis_size("members")
    half_lats = lat_total // 2
    upper = degrees // 2

    def remote(src, dst, send_sem, recv_sem, peer):
        return pltpu.make_async_remote_copy(
            src_ref=src,
            dst_ref=dst,
            send_sem=send_sem,
            recv_sem=recv_sem,
            device_id=place(peer, level_parts),
            device_id_type=pl.DeviceIdType.MESH,
        )

    def loop(count, body):
        def run(i, carry):
            body(i)
            return carry

        lax.fori_loop(0, count, run, 0)

    def forward(c, peer, landing, cut):
        return remote(
            buf.at[(c, peer, *cut)], land.at[(c, landing, *cut)], fs.at[c, peer], fr.at[c, landing], peer
        )

    def forward_own(c, cut):
        return pltpu.make_async_copy(buf.at[(c, mine, *cut)], land.at[(c, mine, *cut)], loc.at[0, c])

    def backward(c, peer, landing):
        return remote(buf.at[c, peer], back.at[c, landing], bs.at[c, peer], br.at[c, landing], peer)

    def backward_own(c):
        return pltpu.make_async_copy(buf.at[c, mine], back.at[c, mine], loc.at[1, c])

    def in_turn(start):
        def one(t):
            turn = (lat + t // level_parts + (1 - sub) * (lat_parts // 2)) % lat_parts
            peer = turn * level_parts + (group + t) % level_parts

            @pl.when(peer != mine)
            def _():
                start(peer)

        loop(n, one)

    def others(wait):
        loop(n - 1, lambda d: wait((mine + 1 + d) % n))

    def push(c, cut):
        in_turn(lambda peer: forward(c, peer, mine, cut).start())
        forward_own(c, cut).start()

    def narrow(o, kind, place_in):
        return remote(
            buf.at[0, o], land_t.at[kind, place_in], ts.at[o], tr.at[kind, place_in], half * half_n + o % half_n
        )

    def narrow_own(kind):
        owner = ((half + kind) % 2) * half_n + seat
        return pltpu.make_async_copy(buf.at[0, owner], land_t.at[kind, seat], loc.at[2, kind])

    def narrow_back(kind, to, owner):
        return remote(
            buf.at[0, kind * half_n + to], back.at[0, owner], bs.at[0, kind * half_n + to], br.at[0, owner],
            half * half_n + to,
        )

    def narrow_back_own(kind):
        owner = ((half + kind) % 2) * half_n + seat
        return pltpu.make_async_copy(buf.at[0, kind * half_n + seat], back.at[0, owner], loc.at[3, kind])

    def seats(do):
        def one(d):
            do((seat + 1 + d) % half_n)

        loop(half_n - 1, one)

    def trig(a):
        return far[0, :, a : a + 1] * cosine[...] - far[1, :, a : a + 1] * sine[...]

    def fetch(i):
        slot = i % 2
        cut = pl.ds(i * STEP, STEP)
        return (
            pltpu.make_async_copy(state.at[cut], st.at[slot], ins.at[0, slot]),
            pltpu.make_async_copy(forcing.at[cut], fo.at[slot], ins.at[1, slot]),
        )

    sibling = mine + 1 - 2 * sub
    high_part = basis.at[:, :, pl.ds(upper, upper)]
    first, second = pl.ds(0, slots), pl.ds(slots, slots)
    weights = (
        pltpu.make_async_copy(basis.at[:, :, pl.ds(0, upper)], low_v, ins.at[2, 0]),
        pltpu.make_async_copy(high_part, high_v.at[first], ins.at[3, 0]),
        pltpu.make_async_copy(solver, solver_v.at[first], ins.at[2, 1]),
        remote(high_part, high_v.at[second], hs.at[0], hr.at[0], sibling),
        remote(solver, solver_v.at[second], hs.at[1], hr.at[1], sibling),
    )

    for copy in fetch(0):
        copy.start()
    barrier = pltpu.get_barrier_semaphore()
    others(
        lambda peer: pl.semaphore_signal(
            barrier, inc=1, device_id=place(peer, level_parts), device_id_type=pl.DeviceIdType.MESH
        )
    )
    def twin(d):
        return dict(place(mine, level_parts), members=(member + d) % members)

    if cap:
        for d in range(1, members):
            pl.semaphore_signal(
                barrier, inc=1, device_id=twin(d), device_id_type=pl.DeviceIdType.MESH
            )
    greeted = n - 1 + (members - 1 if cap else 0)
    for a in range(lons // tile):
        table[:, a * tile : (a + 1) * tile] = trig(a).astype(jnp.bfloat16)

    lead = 1 if cap else 0

    def dft(i):
        for copy in fetch(i):
            copy.wait()

        @pl.when(i + 1 < steps)
        def _():
            for copy in fetch(i + 1):
                copy.start()

        slot = i % 2
        present = st[slot].astype(jnp.float32)
        explicit = (
            present
            + 0.5 * fo[slot].astype(jnp.float32)
            - 0.3 * present * present * present / (1.0 + present * present)
        ).astype(jnp.bfloat16)
        spectral = lax.dot_general(
            table[...],
            explicit.reshape(STEP * lats, lons),
            (((1,), (1,)), ((), ())),
            preferred_element_type=jnp.float32,
        ).astype(jnp.bfloat16)
        spectral = spectral.reshape(chunks, n, pairs, STEP * lats)
        for level in range(STEP):
            buf[:, :, i * STEP + level] = spectral[..., level * lats : (level + 1) * lats]

        @pl.when(i == 0)
        def _():
            pl.semaphore_wait(barrier, greeted)
            for copy in weights:
                copy.start()

        push(lead, (pl.ds(i * STEP, STEP),))

    loop(steps, dft)
    for copy in weights:
        copy.wait()

    if cap:
        lanes = packed.shape[1]
        place_of = lax.broadcasted_iota(jnp.int32, (upper, lanes), 0)
        packed[...] = jnp.zeros_like(packed)

        def pack(w):
            pick = (place_of + w * upper == key[...]).astype(jnp.float32).astype(jnp.bfloat16)
            part = jnp.dot(
                high_v[order[w]], pick, preferred_element_type=jnp.float32
            )
            packed[...] = (packed[...].astype(jnp.float32) + part).astype(jnp.bfloat16)

        loop(GROUP, pack)
        share = half_lats // members
        far_share = pl.ds(pl.multiple_of((1 - half) * half_lats + member * share, share), share)
        near_rows = pl.ds(pl.multiple_of(half * half_lats, half_lats), half_lats)
        give_rows = remote(packed.at[far_share], given, ms.at[0], mr.at[0], mirror)
        give_rows.start()

        def narrow_start(d):
            o = (mine + half_n + d) % n

            @pl.when(o % half_n != seat)
            def _():
                narrow(o, (o // half_n + half) % 2, seat).start()

        loop(n, narrow_start)
        for kind in range(2):
            narrow_own(kind).start()
    for c in range(lead + 1, chunks):
        push(c, ())

    for a in range(lons // tile):
        table[:, a * tile : (a + 1) * tile] = (trig(a) * far[2, :, a : a + 1]).astype(jnp.bfloat16)
    give_table = pltpu.make_async_copy(table, synthesis, loc.at[4, 0])
    give_table.start()

    def take(source, bands):
        landed = pltpu.make_async_copy(source, got.at[pl.ds(0, bands * level_parts)], loc.at[4, 1])
        landed.start()
        landed.wait()

        def gather(q):
            at = pl.ds(pl.multiple_of(q * lats, lats), lats)
            for g in range(level_parts):
                wide[g] = got[q * level_parts + g].astype(jnp.float32).reshape(levels * pairs, lats)
                for k in range(pairs):
                    rows[k, pl.ds(g * levels, levels), at] = wide[g, pl.ds(k, levels, stride=pairs), :]

        loop(bands, gather)

    def spread(s, bands):
        for q in range(bands):
            for g in range(level_parts):
                for c in range(2):
                    split[q * level_parts + g, pl.ds(2 * s + c, levels, stride=pairs), :] = mix[
                        pl.ds(c * total + g * levels, levels), q * lats : (q + 1) * lats
                    ]

    def whole(c):
        others(lambda peer: forward(c, mine, peer, ()).wait_recv())
        forward_own(c, ()).wait()
        take(land.at[c], lat_parts)
        low = upper if c < slots // 2 // GROUP else 0

        def slot(s):
            here = order[c * GROUP + s]
            legendre = high_v[here]
            if not low:
                legendre = jnp.concatenate([low_v[here], legendre], axis=1)
            columns = rows[pl.ds(2 * s, 2)].reshape(2 * total, lat_total).astype(jnp.bfloat16)
            coeffs = jnp.dot(columns, legendre, preferred_element_type=jnp.float32)
            mask = alive[c * GROUP + s][:, low:] > 0.5
            solved = []
            for k in range(2):
                part = coeffs[k * total : (k + 1) * total].astype(jnp.bfloat16)
                part = jnp.dot(solver_v[here], part, preferred_element_type=jnp.float32)
                solved.append(jnp.where(mask, part, 0.0))
            solved = jnp.concatenate(solved, axis=0).astype(jnp.bfloat16)
            mix[...] = lax.dot_general(
                solved, legendre, (((1,), (1,)), ((), ())), preferred_element_type=jnp.float32
            )
            spread(s, lat_parts)

        loop(GROUP, slot)
        others(lambda peer: forward(c, peer, mine, ()).wait_send())

        def fill(peer):
            buf[c, peer] = split[peer].astype(jnp.bfloat16).reshape(levels, pairs, lats)

        fill(mine)
        backward_own(c).start()

        def send(peer):
            fill(peer)
            backward(c, peer, mine).start()

        in_turn(send)

    def narrow_coeffs(kind, legendre):
        seats(lambda j: narrow(j, kind, j).wait_recv())
        narrow_own(kind).wait()
        take(land_t.at[kind], lat_parts // 2)
        acc[...] = jnp.zeros_like(acc)

        def one(w):
            columns = rows[pl.ds(2 * w, 2), :, :half_lats].reshape(2 * total, half_lats).astype(jnp.bfloat16)
            part = jnp.dot(columns, legendre(), preferred_element_type=jnp.float32)
            acc[...] = jnp.where(who[kind] == w, part, acc[...])

        loop(GROUP, one)

    def narrow_synthesis(kind, source, legendre):
        def one(w):
            solved = jnp.where(who[kind] == w, source[...].astype(jnp.float32), 0.0).astype(jnp.bfloat16)
            mix[:, :half_lats] = lax.dot_general(
                solved, legendre(), (((1,), (1,)), ((), ())), preferred_element_type=jnp.float32
            )
            spread(w, lat_parts // 2)

        loop(GROUP, one)

        def fill(j):
            buf[0, kind * half_n + j] = split[j].astype(jnp.bfloat16).reshape(levels, pairs, lats)

        owner = mine if kind == 0 else mirror
        fill(seat)
        narrow_back_own(kind).start()

        def send(j):
            fill(j)
            narrow_back(kind, j, owner).start()

        seats(send)

    if cap:
        give_part = remote(part_out, part_in, ms.at[1], mr.at[1], mirror)
        give_solved = remote(solved_out, solved_in, ms.at[2], mr.at[2], mirror)
        whole(1)
        give_rows.wait_recv()

        def pass_rows(d):
            return pltpu.make_async_remote_copy(
                src_ref=given,
                dst_ref=passed.at[d - 1],
                send_sem=ms.at[2 + d],
                recv_sem=mr.at[2 + d],
                device_id=twin(d),
                device_id_type=pl.DeviceIdType.MESH,
            )

        def keep_rows(part, value):
            other[pl.ds(pl.multiple_of(part * share, share), share)] = value

        for d in range(1, members):
            pass_rows(d).start()
        keep_rows(member, given[...])
        for d in range(1, members):
            pass_rows(d).wait()
            keep_rows((member + members - d) % members, passed[d - 1])

        narrow_coeffs(1, lambda: other[...])
        part_out[...] = acc[...].astype(jnp.bfloat16)
        give_part.start()
        whole(2)
        narrow_coeffs(0, lambda: packed[near_rows])
        give_part.wait_recv()
        acc[...] += part_in[...].astype(jnp.float32)

        def solve(w):
            for k in range(2):
                at = pl.ds(k * total, total)
                part = jnp.dot(
                    solver_v[order[w]], acc[at].astype(jnp.bfloat16), preferred_element_type=jnp.float32
                )
                split_at = who[0] == w
                solved_f[at] = jnp.where(split_at, part, solved_f[at])

        solved_f[...] = jnp.zeros_like(solved_f)
        loop(GROUP, solve)
        solved_out[...] = solved_f[...].astype(jnp.bfloat16)
        give_solved.start()

        def narrow_sent(d):
            o = (mine + half_n + d) % n

            @pl.when(o % half_n != seat)
            def _():
                narrow(o, (o // half_n + half) % 2, seat).wait_send()

        loop(n, narrow_sent)
        narrow_synthesis(0, solved_out, lambda: packed[near_rows])
        for c in range(3, chunks):
            whole(c)
        give_solved.wait_recv()
        narrow_synthesis(1, solved_in, lambda: other[...])
        for copy in (give_rows, give_part, give_solved):
            copy.wait_send()
        for kind in range(2):
            owner = mine if kind == 0 else mirror
            narrow_back_own(kind).wait()
            seats(lambda j, kind=kind, owner=owner: narrow_back(kind, j, owner).wait_send())

            def arrived(j, kind=kind):
                narrow_back(kind, j, ((half + kind) % 2) * half_n + j).wait_recv()

            seats(arrived)
    else:
        for c in range(chunks):
            whole(c)
    for c in range(lead, chunks):
        others(lambda peer, c=c: backward(c, peer, mine).wait_send())
        others(lambda peer, c=c: backward(c, mine, peer).wait_recv())
        backward_own(c).wait()
    give_table.wait()


def fused(state, forcing, basis, solver, cosine, sine, far, alive, order, key, who, n, level_parts, cap, number):
    levels, lats, lons = state.shape
    slots, lat_total, degrees = basis.shape
    total = solver.shape[1]
    pairs = 2 * GROUP
    chunks = slots // GROUP
    table_rows = cosine.shape[0]
    lanes = cap if cap else 128
    half_lats = lat_total // 2
    members = lax.axis_size("members")
    some = lambda *shape: shape if cap else (16, 128)
    message = (levels, pairs, lats)
    vmem = pl.BlockSpec(memory_space=pltpu.VMEM)
    hbm = pl.BlockSpec(memory_space=pl.ANY)
    smem = pl.BlockSpec(memory_space=pltpu.SMEM)
    short = (16, 16, 128)
    bf16, f32 = jnp.bfloat16, jnp.float32
    _, _, back, synthesis = pl.pallas_call(
        functools.partial(fused_kernel, n, level_parts, cap),
        out_shape=(
            jax.ShapeDtypeStruct((chunks, n, *message), bf16),
            jax.ShapeDtypeStruct((2, n // 2, *(message if cap else short)), bf16),
            jax.ShapeDtypeStruct((chunks, n, *message), bf16),
            jax.ShapeDtypeStruct((table_rows, lons), bf16),
        ),
        in_specs=[hbm, hbm, hbm, hbm, vmem, vmem, vmem, vmem, smem, vmem, vmem],
        out_specs=(hbm, hbm, hbm, hbm),
        scratch_shapes=[
            pltpu.VMEM((table_rows, lons), bf16),
            pltpu.VMEM((chunks, n, *message), bf16),
            pltpu.VMEM((slots, lat_total, degrees // 2), bf16),
            pltpu.VMEM((2 * slots, lat_total, degrees // 2), bf16),
            pltpu.VMEM((2 * slots, total, total), bf16),
            pltpu.VMEM((n, *message), bf16),
            pltpu.VMEM((level_parts, levels * pairs, lats), f32),
            pltpu.VMEM((pairs, total, lat_total), f32),
            pltpu.VMEM((2 * total, lat_total), f32),
            pltpu.VMEM((n, levels * pairs, lats), f32),
            pltpu.VMEM((2, STEP, lats, lons), bf16),
            pltpu.VMEM((2, STEP, lats, lons), bf16),
            pltpu.VMEM(some(lat_total, lanes), bf16),
            pltpu.VMEM(some(half_lats // members, lanes), bf16),
            pltpu.VMEM((max(members - 1, 1), *some(half_lats // members, lanes)), bf16),
            pltpu.VMEM(some(half_lats, lanes), bf16),
            pltpu.VMEM(some(2 * total, lanes), f32),
            pltpu.VMEM(some(2 * total, lanes), f32),
            pltpu.VMEM(some(2 * total, lanes), bf16),
            pltpu.VMEM(some(2 * total, lanes), bf16),
            pltpu.VMEM(some(2 * total, lanes), bf16),
            pltpu.VMEM(some(2 * total, lanes), bf16),
            pltpu.SemaphoreType.DMA((chunks, n)),
            pltpu.SemaphoreType.DMA((chunks, n)),
            pltpu.SemaphoreType.DMA((chunks, n)),
            pltpu.SemaphoreType.DMA((chunks, n)),
            pltpu.SemaphoreType.DMA((n,)),
            pltpu.SemaphoreType.DMA((2, n // 2)),
            pltpu.SemaphoreType.DMA((2 + members,)),
            pltpu.SemaphoreType.DMA((2 + members,)),
            pltpu.SemaphoreType.DMA((2,)),
            pltpu.SemaphoreType.DMA((2,)),
            pltpu.SemaphoreType.DMA((5, max(chunks, 2))),
            pltpu.SemaphoreType.DMA((4, 2)),
        ],
        compiler_params=pltpu.CompilerParams(
            collective_id=number, has_side_effects=True, vmem_limit_bytes=63 << 20
        ),
    )(state, forcing, basis, solver, cosine, sine, far, alive, order, key, who)
    return back, synthesis

def small_tables(waves, lon_count, tile):
    waves = jnp.repeat(waves, 2)[:, None]
    quarter = (jnp.arange(waves.shape[0], dtype=jnp.int32) % 2)[:, None] * (lon_count // 4)
    unit = 2.0 * math.pi / lon_count
    fine = jnp.arange(tile, dtype=jnp.int32)[None, :] * waves % lon_count
    coarse = jnp.arange(lon_count // tile, dtype=jnp.int32)[None, :] * tile * waves + quarter
    fine, coarse = fine.astype(jnp.float32) * unit, (coarse % lon_count).astype(jnp.float32) * unit
    factor = 1.0 / math.sqrt(lon_count)
    weights = jnp.broadcast_to(jnp.where(waves == 0, 1.0, 2.0), coarse.shape)
    far = jnp.stack([jnp.cos(coarse) * factor, jnp.sin(coarse) * factor, weights])
    return jnp.cos(fine), jnp.sin(fine), far


def slot_order(waves, n):
    chips = waves.reshape(n // 2, -1)
    both = chips.shape[1]
    slots = both // 2
    source = jnp.arange(both, dtype=jnp.int32)
    above = chips[:, None, :] > chips[:, :, None]
    beside = source[:, None] // slots == source // slots
    rank = jnp.sum(above.astype(jnp.int32), axis=2)
    own = jnp.sum((above & beside).astype(jnp.int32), axis=2)
    core = (rank + 1) // 2 % 2
    to = jnp.where(rank < slots, core * slots + rank // 2, source // slots * slots + own)
    here = to[:, :, None] == source
    ranked = jnp.sum(jnp.where(here, chips[:, :, None], 0), axis=1).reshape(n, slots)
    order = jnp.sum(jnp.where(here, source[None, :, None], 0), axis=1).reshape(n // 2, 2, slots)
    order = (order + jnp.arange(2, dtype=jnp.int32)[:, None] * slots) % both
    return ranked, order.reshape(n, slots)


def packing(ranked, degrees, lanes):
    first = ranked[:, :GROUP]
    counts = degrees - first
    before = jnp.arange(GROUP)[:, None] > jnp.arange(GROUP)[None, :]
    starts = jnp.sum(jnp.where(before, counts[:, None, :], 0), axis=2)
    lane = jnp.arange(lanes, dtype=jnp.int32)
    inside = (lane >= starts[:, :, None]) & (lane < (starts + counts)[:, :, None])
    upper = degrees // 2
    wave = jnp.arange(GROUP, dtype=jnp.int32)[None, :, None]
    column = wave * upper + first[:, :, None] - upper + lane - starts[:, :, None]
    key = jnp.sum(jnp.where(inside, column + 1, 0), axis=1) - 1
    who = jnp.sum(jnp.where(inside, wave + 1, 0), axis=1) - 1
    return key, who


def fast(state, forcing, basis, solver, waves, lat_parts, level_parts):
    levels, lats, lons = state.shape
    slots, _, degrees = basis.shape
    n = lat_parts * level_parts
    chunks = slots // GROUP
    owner = lax.axis_index(OWNERS)

    mirror = (owner + n // 2) % n
    ranked, order = slot_order(waves, n)
    flat = ranked.reshape(n, chunks, GROUP).transpose(1, 0, 2).reshape(-1)
    cosine, sine, far = small_tables(flat, lons, 128)
    mine = lax.dynamic_index_in_dim(ranked, owner, 0, keepdims=False)
    live = jnp.arange(degrees, dtype=jnp.int32)[None, :] >= mine[:, None]
    alive = live.astype(jnp.float32)[:, None, :]
    order = lax.dynamic_index_in_dim(order, owner, 0, keepdims=False)

    def branch(number):
        cap = CAPS[number]

        def run(operands):
            both = jnp.stack(
                [lax.dynamic_index_in_dim(ranked, o, 0, keepdims=False) for o in (owner, mirror)]
            )
            key, who = packing(both, degrees, max(cap, 128))
            return fused(*operands, key[:1], who[:, None], n, level_parts, cap, number)

        return run

    needed = jnp.max(jnp.sum(degrees - ranked[:, :GROUP], axis=1))
    unfit = sum((needed > cap).astype(jnp.int32) for cap in CAPS if cap)
    back, synthesis = lax.switch(
        unfit,
        [branch(number) for number in range(len(CAPS))],
        (state, forcing, basis, solver, cosine, sine, far, alive, order),
    )
    synthesis = synthesis.reshape(chunks, n, 2 * GROUP, lons)
    result = jnp.einsum("holkx,hokj->lxj", back, synthesis, preferred_element_type=jnp.float32)
    return result.astype(jnp.bfloat16)


def make_shards(lat_parts, level_parts):
    owners = lat_parts * level_parts

    def shards(state, forcing, basis, solver, waves):
        levels, lats, lons = state.shape
        slots, lat_total, degrees = basis.shape
        level_total = solver.shape[1]
        owner = lax.axis_index(OWNERS)
        my_waves = lax.dynamic_slice_in_dim(waves, owner * slots, slots)
        live = jnp.arange(degrees, dtype=jnp.int32)[None, :] >= my_waves[:, None]
        if (
            lats % 128 == 0
            and lons % 512 == 0
            and slots == 4 * GROUP
            and lax.axis_size("sub") == 2
            and levels % STEP == 0
            and lat_parts % 2 == 0
        ):
            return fast(state, forcing, basis, solver, waves, lat_parts, level_parts)
        present = state.astype(jnp.float32)
        explicit = (
            present
            + 0.5 * forcing.astype(jnp.float32)
            - 0.3 * present * present * present / (1.0 + present * present)
        ).astype(jnp.bfloat16)
        raw = raw_table(waves, lons)
        analysis = raw.astype(jnp.bfloat16)
        weights = jnp.where(waves == 0, 1.0, 2.0).astype(jnp.float32)
        synthesis = (raw * weights[:, None, None]).astype(jnp.bfloat16)
        chunks = CHUNKS
        part = slots // chunks
        analysis = analysis.reshape(owners, slots, 2, lons)
        synthesis = synthesis.reshape(owners, slots, 2, lons)
        sent = []
        for i in range(chunks):
            own = slice(i * part, (i + 1) * part)
            spectral = jnp.einsum(
                "oscj,lxj->osclx", analysis[:, own], explicit, preferred_element_type=jnp.float32
            ).astype(jnp.bfloat16)
            sent.append(lax.all_to_all(spectral, OWNERS, split_axis=0, concat_axis=0, tiled=True))
        back = []
        for i in range(chunks):
            own = slice(i * part, (i + 1) * part)
            got = sent[i].reshape(lat_parts, level_parts, part, 2, levels, lats)
            table = basis[own]
            columns = got.transpose(2, 3, 1, 4, 0, 5).reshape(part, 2 * level_total, lat_total)
            coeffs = jnp.einsum(
                "srx,sxn->srn", columns, table, preferred_element_type=jnp.float32
            ).astype(jnp.bfloat16).reshape(part, 2, level_total, degrees)
            solved = jnp.einsum(
                "skl,scln->sckn", solver[own], coeffs, preferred_element_type=jnp.float32
            )
            solved = jnp.where(live[own][:, None, None, :], solved, 0.0).astype(jnp.bfloat16)
            grid = jnp.einsum(
                "srn,sxn->srx",
                solved.reshape(part, 2 * level_total, degrees),
                table,
                preferred_element_type=jnp.float32,
            ).astype(jnp.bfloat16)
            grid = grid.reshape(part, 2, level_parts, levels, lat_parts, lats)
            grid = grid.transpose(4, 2, 0, 1, 3, 5).reshape(owners, part, 2, levels, lats)
            back.append(lax.all_to_all(grid, OWNERS, split_axis=0, concat_axis=0, tiled=True))
        waved = jnp.concatenate(back, axis=1)
        result = jnp.einsum(
            "osclx,oscj->lxj", waved, synthesis, preferred_element_type=jnp.float32
        )
        return result.astype(jnp.bfloat16)

    return shards


def solution(mesh):
    lat_parts = mesh.shape["lat"]
    level_parts = mesh.shape["lev"] * mesh.shape["sub"]
    return jax.shard_map(
        make_shards(lat_parts, level_parts),
        mesh=mesh,
        in_specs=(
            P(("members", "lev", "sub"), "lat", None),
            P(("members", "lev", "sub"), "lat", None),
            P(OWNERS, None, None),
            P(OWNERS, None, None),
            P(),
        ),
        out_specs=P(("members", "lev", "sub"), "lat", None),
        check_vma=False,
    )
```
